512 devices in a mesh: tm: 16 (over y, x_lo, core), strip: 32 (over z, x_hi).
Axes of the slice: x: 4 (x_hi: 2, x_lo: 2; x = x_hi * 2 + x_lo), y: 4, z: 16, core: 2. Of those that a mesh axis runs over, the one named last changes fastest.
Arguments:
- increment: float32 [16, 3, 1024, 384], P('tm', None, 'strip'), may hold values from -6 to 6
- ref_depth: float32 [16, 1, 1024, 384], P('tm', None, 'strip'), may hold values from 0.6 to 1.4
- ref_wind: float32 [16, 2, 1024, 384], P('tm', None, 'strip'), may hold values from -0.5 to 0.5
- spread: float32 [16, 3, 1024, 384], P('tm', None, 'strip'), may hold values from 0.5 to 2
- decay: float32 [16, 3, 1024, 384], P('tm', None, 'strip'), may hold values from 0.3 to 0.97
Outputs:
- product: float32 [16, 3, 1024, 384], P('tm', None, 'strip')
The draws below stay inside these ranges and needn't reach their ends.
All inputs are finite; a program needn't handle non-finite values.
Results may differ from the reference program's by a relative error of at most 0.00011.
Values sent between devices are 32-bit elements; how exact they have to be, the bound alone decides.
A program may use at most 64 MiB of HBM per device.

```python
import math
import jax
import jax.numpy as jnp
from jax import lax

COLS = 384
STEPS = 12
SUBWIN = 16
NY = 1024


def level_of(stream_key, dims, split, smallest, largest):
    loudness, own = 1.0, jax.random.fold_in(stream_key, 6)
    for position, shards_of in split:
        steps = jnp.exp(jax.random.uniform(jax.random.fold_in(own, position), (shards_of,), jnp.float32, smallest / len(split), largest / len(split)))
        loudness = loudness * jnp.repeat(steps, dims[position] // shards_of).reshape([-1 if axis == position else 1 for axis in range(len(dims))])
    return loudness


def gaussian(own_key, dims, scale, reach, cuts=(), kind=jnp.bfloat16):
    drawn = scale * jax.random.normal(own_key, dims, jnp.float32)
    if cuts:
        drawn = drawn * level_of(own_key, dims, cuts, -0.22, 0.18)
    return jnp.clip(drawn, -reach, reach).astype(kind)


def setup_inputs(seed: int = 0) -> dict:
    key_list = jax.random.split(jax.random.key(seed), 6)
    increment = gaussian(key_list[0], (SUBWIN, 3, NY, COLS), 1.0, 6.0, ((0, 16), (2, 32)), jnp.float32)
    ref_depth = jnp.clip(0.6 + 0.79999995 * jax.random.uniform(key_list[1], (SUBWIN, 1, NY, COLS), jnp.float32) ** level_of(key_list[1], (SUBWIN, 1, NY, COLS), ((0, 16), (2, 32)), -0.2, 0.2), 0.6, 1.4)
    ref_wind = jnp.clip(jax.random.uniform(key_list[2], (SUBWIN, 2, NY, COLS), jnp.float32, -0.5, 0.5) * level_of(key_list[2], (SUBWIN, 2, NY, COLS), ((0, 16), (2, 32)), -0.4, 0.0), -0.5, 0.5)
    spread = jnp.clip(jnp.exp(math.log(2.0) - 1.3862944 * jax.random.uniform(key_list[3], (SUBWIN, 3, NY, COLS), jnp.float32) ** level_of(key_list[3], (SUBWIN, 3, NY, COLS), ((0, 16), (2, 32)), -0.2, 0.2)), 0.5, 2.0)
    decay = jnp.clip(0.3 + 0.67 * jax.random.uniform(key_list[4], (SUBWIN, 3, NY, COLS), jnp.float32) ** level_of(key_list[4], (SUBWIN, 3, NY, COLS), ((0, 16), (2, 32)), -0.2, 0.2), 0.3, 0.97)
    return {"increment": increment, "ref_depth": ref_depth, "ref_wind": ref_wind, "spread": spread, "decay": decay}


time_step = 0.4
gravity = 1.0

def inner(field):
    return field[..., 1:-1, :]

def along_x(field):
    return (0.5 * (jnp.roll(field, -1, -1) - jnp.roll(field, 1, -1)))[..., 1:-1, :]

def along_y(field):
    return 0.5 * (field[..., 2:, :] - field[..., :-2, :])

def model_step(padded, ref_padded, first_row, total_rows):
    height = padded[..., 0, :, :]
    east_flow = padded[..., 1, :, :]
    north_flow = padded[..., 2, :, :]
    depth_ref = ref_padded[..., 0, :, :]
    east_ref = ref_padded[..., 1, :, :]
    north_ref = ref_padded[..., 2, :, :]
    out_rows = padded.shape[-2] - 2
    row_ids = first_row + jnp.arange(out_rows, dtype=jnp.int32)
    coriolis = (0.2 + 0.4 * row_ids.astype(jnp.float32) / total_rows)[:, None]
    inside = ((row_ids >= 0) & (row_ids < total_rows)).astype(jnp.float32)[:, None]
    flux_east = depth_ref * east_flow + east_ref * height
    flux_north = depth_ref * north_flow + north_ref * height
    new_height = inner(height) - time_step * (along_x(flux_east) + along_y(flux_north))
    new_east = inner(east_flow) - time_step * (inner(east_ref) * along_x(east_flow) + inner(north_ref) * along_y(east_flow) + gravity * along_x(height) - coriolis * inner(north_flow))
    new_north = inner(north_flow) - time_step * (inner(east_ref) * along_x(north_flow) + inner(north_ref) * along_y(north_flow) + gravity * along_y(height) + coriolis * inner(east_flow))
    return jnp.stack([new_height, new_east, new_north], axis=-3) * inside

def pad_rows(field, width):
    return jnp.pad(field, ((0, 0), (0, 0), (width, width), (0, 0)))

def propagate(fields, ref_padded):
    for repeat in range(STEPS):
        fields = model_step(pad_rows(fields, 1), ref_padded, 0, NY)
    return fields

def reference(increment, ref_depth, ref_wind, spread, decay):
    references = jnp.concatenate([ref_depth, ref_wind], axis=1)
    ref_padded = pad_rows(references, 1)
    tangent = propagate(increment, ref_padded)
    carried = jnp.concatenate([jnp.zeros_like(tangent[:1]), tangent[:-1]], axis=0)
    residual = increment - carried
    scaled = spread * residual

    def forward(carry, element):
        built = element[1] * carry + element[0]
        return (built, built)
    _, built_all = lax.scan(forward, jnp.zeros_like(scaled[0]), (scaled, decay))

    def backward(carry, element):
        smoothed = element[0] + carry
        return (element[1] * smoothed, smoothed)
    _, smoothed_all = lax.scan(backward, jnp.zeros_like(scaled[0]), (built_all, decay), reverse=True)
    weighted = spread * smoothed_all
    following = jnp.concatenate([weighted[1:], jnp.zeros_like(weighted[:1])], axis=0)
    _, pullback = jax.vjp(lambda fields: propagate(fields, ref_padded), jnp.zeros_like(weighted))
    adjoint = pullback(following)[0]
    return weighted - adjoint
```

```python
import functools

import jax
import jax.numpy as jnp
from jax import lax
from jax.experimental import pallas as pl
from jax.experimental.pallas import tpu as pltpu
from jax.sharding import PartitionSpec as P

STEPS = 12
DT = 0.4
HALF = 0.5 * DT
LANES = 128
TOP = 24
MESH = pl.DeviceIdType.MESH


def lane_masks(shape):
    lane = lax.broadcasted_iota(jnp.int32, shape, len(shape) - 1)
    return lane == 0, lane == LANES - 1


def cycle(x, by):
    return jnp.concatenate([x[by:], x[:by]], axis=0)


def diff_x(f, masks):
    first, last = masks
    ahead = pltpu.roll(f, LANES - 1, 2)
    behind = pltpu.roll(f, 1, 2)
    return jnp.where(last, cycle(ahead, 1), ahead) - jnp.where(first, cycle(behind, -1), behind)


def tangent_step(src, dst, ref, tmp, fc, first, stop, keep_low, keep_high):
    cols = src.shape[0] // 3
    masks = lane_masks((cols, 8, LANES))
    for t in range(first - 1, stop + 1):
        rows = pl.ds(8 * t, 8)
        tmp[0:cols, rows] = (
            ref[0:cols, rows] * src[2 * cols :, rows] + ref[2 * cols :, rows] * src[0:cols, rows]
        )
    for t in range(first, stop):
        rows, below, above = (pl.ds(8 * t + d, 8) for d in (0, -1, 1))
        h, u, v = (src[i * cols : (i + 1) * cols, rows] for i in range(3))
        depth, east, north = (ref[i * cols : (i + 1) * cols, rows] for i in range(3))
        turn = fc[rows][None]

        def diff_y(buf, i):
            return buf[i * cols : (i + 1) * cols, above] - buf[i * cols : (i + 1) * cols, below]

        flux = depth * u + east * h
        new_h = h - (diff_x(flux, masks) + diff_y(tmp, 0))
        new_u = u - ((east * diff_x(u, masks) + north * diff_y(src, 1)) + (diff_x(h, masks) - turn * v))
        new_v = v - ((east * diff_x(v, masks) + north * diff_y(src, 2)) + (diff_y(src, 0) + turn * u))
        for i, new in enumerate((new_h, new_u, new_v)):
            if t == TOP // 8 - 1:
                new = jnp.where(keep_low, new, 0.0)
            if t == TOP // 8 + 4:
                new = jnp.where(keep_high, new, 0.0)
            dst[i * cols : (i + 1) * cols, rows] = new


def adjoint_step(src, dst, ref, tmp, fc, first, stop, keep_low, keep_high):
    cols = src.shape[0] // 3
    masks = lane_masks((cols, 8, LANES))
    for t in range(first - 1, stop + 1):
        rows = pl.ds(8 * t, 8)
        north = ref[2 * cols :, rows]
        tmp[0:cols, rows] = north * src[cols : 2 * cols, rows]
        tmp[cols : 2 * cols, rows] = north * src[2 * cols :, rows]
    for t in range(first, stop):
        rows, below, above = (pl.ds(8 * t + d, 8) for d in (0, -1, 1))
        p, q, s = (src[i * cols : (i + 1) * cols, rows] for i in range(3))
        depth, east, north = (ref[i * cols : (i + 1) * cols, rows] for i in range(3))
        turn = fc[rows][None]

        def diff_y(buf, i):
            return buf[i * cols : (i + 1) * cols, above] - buf[i * cols : (i + 1) * cols, below]

        px, py = diff_x(p, masks), diff_y(src, 0)
        new_p = p + ((east * px + north * py) + (diff_x(q, masks) + diff_y(src, 2)))
        new_q = q + ((depth * px - turn * s) + (diff_x(east * q, masks) + diff_y(tmp, 0)))
        new_s = s + ((depth * py + turn * q) + (diff_x(east * s, masks) + diff_y(tmp, 1)))
        for i, new in enumerate((new_p, new_q, new_s)):
            if t == TOP // 8 - 1:
                new = jnp.where(keep_low, new, 0.0)
            if t == TOP // 8 + 4:
                new = jnp.where(keep_high, new, 0.0)
            dst[i * cols : (i + 1) * cols, rows] = new


def run_steps(step, a, b):
    lo = TOP // 8
    step(a, b, lo - 2, lo + 6)
    step(b, a, lo - 2, lo + 6)
    step(a, b, lo - 2, lo + 6)

    def pair(_, carry):
        step(b, a, lo - 1, lo + 5)
        step(a, b, lo - 1, lo + 5)
        return carry

    lax.fori_loop(0, 4, pair, 0)
    step(b, a, lo, lo + 4)


def kernel(
    tms, strips, total_rows,
    inc_hbm, depth_hbm, wind_hbm, spread_hbm, decay_hbm, out_ref,
    fa, fb, ref, tmp, fc, spread, decay,
    halo_out, halo_in, pre_out, pre_in, tan_out, tan_in, scan_b, w_own, w_in, wl_in, wh_in, wk_in, wk,
    load_sem, halo_send, halo_recv, pre_send, pre_recv, tan_send, tan_recv,
    w_send, w_recv, wh_send, wl_recv, wh_recv, wk_send, wk_recv,
):
    nine = fa.shape[0]
    cols = nine // 3
    rows = spread.shape[1]
    per = rows // tms
    halo = STEPS
    edge = halo // per
    tm = lax.axis_index("tm")
    strip = lax.axis_index("strip")
    has_low, has_high = strip > 0, strip < strips - 1
    to_low, to_high = jnp.logical_and(has_low, tm < edge), jnp.logical_and(has_high, tm >= tms - edge)

    loads = []

    def load(hbm, planes, buf, base, offset, sem):
        for p in range(planes):
            for c in range(cols):
                copy = pltpu.make_async_copy(
                    hbm.at[0, p, :, pl.ds(c * LANES, LANES)],
                    buf.at[base + p * cols + c, pl.ds(offset, rows)],
                    load_sem.at[sem, p * cols + c],
                )
                copy.start()
                loads.append(copy)

    load(inc_hbm, 3, fa, 0, TOP, 0)
    load(depth_hbm, 1, ref, 0, TOP, 1)
    load(wind_hbm, 2, ref, cols, TOP, 2)
    load(spread_hbm, 3, spread, 0, 0, 3)
    load(decay_hbm, 3, decay, 0, 0, 4)

    barrier = pltpu.get_barrier_semaphore()
    for d in range(1, tms):
        pl.semaphore_signal(barrier, inc=1, device_id=(lax.rem(tm + d, tms), strip), device_id_type=MESH)

    @pl.when(has_low)
    def _():
        pl.semaphore_signal(barrier, inc=1, device_id=(tm, strip - 1), device_id_type=MESH)

    @pl.when(has_high)
    def _():
        pl.semaphore_signal(barrier, inc=1, device_id=(tm, strip + 1), device_id_type=MESH)

    for buf in (fa, fb, ref):
        buf[:, 0:TOP] = jnp.zeros((nine, TOP, LANES), jnp.float32)
        buf[:, TOP + rows :] = jnp.zeros((nine, fa.shape[1] - TOP - rows, LANES), jnp.float32)
    tmp[...] = jnp.zeros_like(tmp)
    row = lax.broadcasted_iota(jnp.int32, fc.shape, 0) + (strip * rows - TOP)
    fc[...] = DT * (0.2 + 0.4 * row.astype(jnp.float32) / total_rows)

    for copy in loads:
        copy.wait()

    for i in range(nine):
        for j in range(tms):
            pre_out[j, 2 * i : 2 * i + per] = fa[i, TOP + per * j : TOP + per * (j + 1)]
            pre_out[j, 18 + 2 * i : 18 + 2 * i + per] = spread[i, per * j : per * (j + 1)]
            pre_out[j, 36 + 2 * i : 36 + 2 * i + per] = decay[i, per * j : per * (j + 1)]

    own = pl.ds(TOP, rows)
    fa[0:cols, own] = fa[0:cols, own] * HALF
    ref[0:cols, own] = ref[0:cols, own] * (HALF * HALF)
    ref[cols:, own] = ref[cols:, own] * HALF

    for i in range(nine):
        for n, buf in ((0, fa), (nine, ref)):
            at = (n + i) * halo
            halo_out[0, at : at + halo] = buf[i, TOP : TOP + halo]
            halo_out[1, at : at + halo] = buf[i, TOP + rows - halo : TOP + rows]

    inside = jnp.logical_and(has_low, has_high)

    @pl.when(inside)
    def _():
        pl.semaphore_wait(barrier, tms + 1)

    @pl.when(jnp.logical_not(inside))
    def _():
        pl.semaphore_wait(barrier, tms)

    to_below = pltpu.make_async_remote_copy(
        halo_out.at[0], halo_in.at[1], halo_send.at[0], halo_recv.at[1],
        device_id=(tm, strip - 1), device_id_type=MESH,
    )
    to_above = pltpu.make_async_remote_copy(
        halo_out.at[1], halo_in.at[0], halo_send.at[1], halo_recv.at[0],
        device_id=(tm, strip + 1), device_id_type=MESH,
    )

    @pl.when(has_low)
    def _():
        to_below.start()

    @pl.when(has_high)
    def _():
        to_above.start()

    def spread_out(out, into, send, recv):
        copies = []
        for d in range(1, tms):
            to = lax.rem(tm + d, tms)
            copies.append(pltpu.make_async_remote_copy(
                out.at[to], into.at[tm], send.at[d], recv.at[tms - d],
                device_id=(to, strip), device_id_type=MESH,
            ))
        for copy in copies:
            copy.start()
        into[tm] = out[tm]
        return copies

    pre_copies = spread_out(pre_out, pre_in, pre_send, pre_recv)

    @pl.when(has_low)
    def _():
        to_above.wait_recv()
        for i in range(nine):
            for n, buf in ((0, fa), (nine, ref)):
                buf[i, TOP - halo : TOP] = halo_in[0, (n + i) * halo : (n + i + 1) * halo]

    @pl.when(has_high)
    def _():
        to_below.wait_recv()
        for i in range(nine):
            for n, buf in ((0, fa), (nine, ref)):
                buf[i, TOP + rows : TOP + rows + halo] = halo_in[1, (n + i) * halo : (n + i + 1) * halo]

    run_steps(
        lambda a, b, first, stop: tangent_step(a, b, ref, tmp, fc, first, stop, has_low, has_high), fa, fb
    )
    for i in range(nine):
        for j in range(tms):
            part = fa[i, TOP + per * j : TOP + per * (j + 1)]
            tan_out[j, per * i : per * (i + 1)] = part * (1.0 / HALF) if i < cols else part

    tan_copies = spread_out(tan_out, tan_in, tan_send, tan_recv)

    for copy in pre_copies:
        copy.wait_recv()
    for copy in tan_copies:
        copy.wait_recv()
    flat = per * nine
    built = None
    for k in range(tms):
        residual = pre_in[k, 0:flat]
        if k:
            residual = residual - tan_in[k - 1]
        scaled = pre_in[k, flat : 2 * flat] * residual
        built = scaled if k == 0 else pre_in[k, 2 * flat :] * built + scaled
        scan_b[k] = built
    w_own[tms] = jnp.zeros((flat, LANES), jnp.float32)
    smoothed = None
    for k in reversed(range(tms)):
        smoothed = scan_b[k] if smoothed is None else scan_b[k] + pre_in[k + 1, 2 * flat :] * smoothed
        w_own[k] = pre_in[k, flat : 2 * flat] * smoothed

    w_copies, low_copies, high_copies, wk_copies = [], [], [], []
    for d in range(tms):
        to = lax.rem(tm + d, tms)
        low_copies.append(pltpu.make_async_remote_copy(
            w_own.at[to + 1], wh_in.at[lax.rem(tm, edge)], wh_send.at[d], wh_recv.at[lax.rem(tm, edge)],
            device_id=(to, strip - 1), device_id_type=MESH,
        ))
        high_copies.append(pltpu.make_async_remote_copy(
            w_own.at[to + 1], wl_in.at[lax.rem(tm + edge - (tms - edge) % edge, edge)], wh_send.at[d],
            wl_recv.at[lax.rem(tm + edge - (tms - edge) % edge, edge)],
            device_id=(to, strip + 1), device_id_type=MESH,
        ))
        if d:
            w_copies.append(pltpu.make_async_remote_copy(
                w_own.at[to + 1], w_in.at[tm], w_send.at[d], w_recv.at[tms - d],
                device_id=(to, strip), device_id_type=MESH,
            ))
            wk_copies.append(pltpu.make_async_remote_copy(
                w_own.at[to], wk_in.at[tm], wk_send.at[d], wk_recv.at[tms - d],
                device_id=(to, strip), device_id_type=MESH,
            ))

    @pl.when(to_low)
    def _():
        for copy in low_copies:
            copy.start()

    @pl.when(to_high)
    def _():
        for copy in high_copies:
            copy.start()

    for copy in w_copies:
        copy.start()
    for copy in wk_copies:
        copy.start()
    w_in[tm] = w_own[tm + 1]
    wk_in[tm] = w_own[tm]

    @pl.when(jnp.logical_not(has_low))
    def _():
        fa[:, 0:TOP] = jnp.zeros((nine, TOP, LANES), jnp.float32)

    @pl.when(jnp.logical_not(has_high))
    def _():
        fa[:, TOP + rows :] = jnp.zeros((nine, fa.shape[1] - TOP - rows, LANES), jnp.float32)

    def unpack(slab, at):
        for i in range(nine):
            part = slab[per * i : per * (i + 1)]
            fa[i, at : at + per] = part * (1.0 / HALF) if i < cols else part

    for copy in w_copies:
        copy.wait_recv()
    for j in range(tms):
        unpack(w_in.at[j], TOP + per * j)

    @pl.when(has_low)
    def _():
        for q in range(edge):
            pltpu.make_async_copy(wl_in.at[q], wl_in.at[q], wl_recv.at[q]).wait()
            unpack(wl_in.at[q], TOP - halo + per * q)

    @pl.when(has_high)
    def _():
        for q in range(edge):
            pltpu.make_async_copy(wh_in.at[q], wh_in.at[q], wh_recv.at[q]).wait()
            unpack(wh_in.at[q], TOP + rows + per * q)

    run_steps(
        lambda a, b, first, stop: adjoint_step(a, b, ref, tmp, fc, first, stop, has_low, has_high), fa, fb
    )
    for copy in wk_copies:
        copy.wait_recv()
    for j in range(tms):
        for i in range(nine):
            wk[i, per * j : per * (j + 1)] = wk_in[j, per * i : per * (i + 1)]
    for i in range(nine):
        adjoint = fa[i, own]
        if i < cols:
            adjoint = adjoint * HALF
        out_ref[0, i // cols, :, (i % cols) * LANES : (i % cols + 1) * LANES] = wk[i] - adjoint

    @pl.when(has_low)
    def _():
        to_below.wait_send()

    @pl.when(has_high)
    def _():
        to_above.wait_send()

    @pl.when(to_low)
    def _():
        for copy in low_copies:
            copy.wait_send()

    @pl.when(to_high)
    def _():
        for copy in high_copies:
            copy.wait_send()

    for copy in pre_copies + tan_copies + w_copies + wk_copies:
        copy.wait_send()


def body(tms, strips, increment, ref_depth, ref_wind, spread, decay):
    _, planes, rows, width = increment.shape
    cols = width // LANES
    nine = planes * cols
    per = rows // tms
    flat = per * nine
    edge = STEPS // per
    height = rows + 2 * TOP
    dma = pltpu.SemaphoreType.DMA
    f32 = jnp.float32
    vmem = lambda *shape: pltpu.VMEM(shape, f32)
    hbm = pl.BlockSpec(memory_space=pl.ANY)
    return pl.pallas_call(
        functools.partial(kernel, tms, strips, strips * rows),
        out_shape=jax.ShapeDtypeStruct(increment.shape, f32),
        in_specs=[hbm] * 5,
        out_specs=pl.BlockSpec(memory_space=pltpu.VMEM),
        scratch_shapes=[
            vmem(nine, height, LANES), vmem(nine, height, LANES), vmem(nine, height, LANES),
            vmem(2 * cols, height, LANES), vmem(height, LANES),
            vmem(nine, rows, LANES), vmem(nine, rows, LANES),
            vmem(2, 2 * nine * STEPS, LANES), vmem(2, 2 * nine * STEPS, LANES),
            vmem(tms, 3 * flat, LANES), vmem(tms, 3 * flat, LANES),
            vmem(tms, flat, LANES), vmem(tms, flat, LANES),
            vmem(tms, flat, LANES), vmem(tms + 1, flat, LANES), vmem(tms, flat, LANES),
            vmem(edge, flat, LANES), vmem(edge, flat, LANES), vmem(tms, flat, LANES),
            vmem(nine, rows, LANES),
            dma((5, nine)), dma((2,)), dma((2,)),
            dma((tms,)), dma((tms,)), dma((tms,)), dma((tms,)),
            dma((tms,)), dma((tms,)), dma((tms,)), dma((edge,)), dma((edge,)), dma((tms,)), dma((tms,)),
        ],
        compiler_params=pltpu.CompilerParams(collective_id=0, has_side_effects=True),
    )(increment, ref_depth, ref_wind, spread, decay)


def solution(mesh):
    spec = P("tm", None, "strip", None)
    return jax.shard_map(
        functools.partial(body, mesh.shape["tm"], mesh.shape["strip"]),
        mesh=mesh,
        in_specs=(spec,) * 5,
        out_specs=spec,
        check_vma=False,
    )
```

```python
import functools

import jax
import jax.numpy as jnp
from jax import lax
from jax.experimental import pallas as pl
from jax.experimental.pallas import tpu as pltpu
from jax.sharding import PartitionSpec as P

STEPS = 12
DT = 0.4
HALF = 0.5 * DT
LANES = 128
TOP = 24
MESH = pl.DeviceIdType.MESH


def diff_x(f):
    after = pltpu.roll(f[:1], LANES - 1, 2)
    before = pltpu.roll(f[-1:], 1, 2)
    return jnp.concatenate([f[1:], after], axis=0) - jnp.concatenate([before, f[:-1]], axis=0)


def third(x):
    return (x * 21846) >> 16


def column_maps(cols):
    lane = lax.broadcasted_iota(jnp.int32, (8, LANES), 1)
    rest = lane - cols * third(lane)
    into, back = [], []
    for j in range(cols):
        x = cols * lane + j
        into.append(x & (LANES - 1))
        block = rest + 2 * j
        block = block - cols * third(block)
        back.append(third(LANES * block + lane - j))
    return (rest == 0, rest == 1), into, back


def choose(marks, parts, j):
    pick = [parts[(2 * j + r) % len(parts)] for r in range(3)]
    return jnp.where(marks[0], pick[0], jnp.where(marks[1], pick[1], pick[2]))


def take_lanes(x, index):
    return jnp.take_along_axis(x, index, axis=1, mode="promise_in_bounds")


def tangent_step(src, dst, ref, tmp, fc, first, stop, keep_low, keep_high):
    cols = src.shape[0] // 3
    for t in range(first - 1, stop + 1):
        rows = pl.ds(8 * t, 8)
        tmp[0:cols, rows] = (
            ref[0:cols, rows] * src[2 * cols :, rows] + ref[2 * cols :, rows] * src[0:cols, rows]
        )
    for t in range(first, stop):
        rows, below, above = (pl.ds(8 * t + d, 8) for d in (0, -1, 1))
        h, u, v = (src[i * cols : (i + 1) * cols, rows] for i in range(3))
        depth, east, north = (ref[i * cols : (i + 1) * cols, rows] for i in range(3))
        turn = fc[rows][None]

        def diff_y(buf, i):
            return buf[i * cols : (i + 1) * cols, above] - buf[i * cols : (i + 1) * cols, below]

        flux = depth * u + east * h
        new_h = h - (diff_x(flux) + diff_y(tmp, 0))
        new_u = u - ((east * diff_x(u) + north * diff_y(src, 1)) + (diff_x(h) - turn * v))
        new_v = v - ((east * diff_x(v) + north * diff_y(src, 2)) + (diff_y(src, 0) + turn * u))
        for i, new in enumerate((new_h, new_u, new_v)):
            if t == TOP // 8 - 1:
                new = jnp.where(keep_low, new, 0.0)
            if t == TOP // 8 + 4:
                new = jnp.where(keep_high, new, 0.0)
            dst[i * cols : (i + 1) * cols, rows] = new


def adjoint_step(src, dst, ref, tmp, fc, first, stop, keep_low, keep_high):
    cols = src.shape[0] // 3
    for t in range(first - 1, stop + 1):
        rows = pl.ds(8 * t, 8)
        north = ref[2 * cols :, rows]
        tmp[0:cols, rows] = north * src[cols : 2 * cols, rows]
        tmp[cols : 2 * cols, rows] = north * src[2 * cols :, rows]
    for t in range(first, stop):
        rows, below, above = (pl.ds(8 * t + d, 8) for d in (0, -1, 1))
        p, q, s = (src[i * cols : (i + 1) * cols, rows] for i in range(3))
        depth, east, north = (ref[i * cols : (i + 1) * cols, rows] for i in range(3))
        turn = fc[rows][None]

        def diff_y(buf, i):
            return buf[i * cols : (i + 1) * cols, above] - buf[i * cols : (i + 1) * cols, below]

        px, py = diff_x(p), diff_y(src, 0)
        new_p = p + ((east * px + north * py) + (diff_x(q) + diff_y(src, 2)))
        new_q = q + ((depth * px - turn * s) + (diff_x(east * q) + diff_y(tmp, 0)))
        new_s = s + ((depth * py + turn * q) + (diff_x(east * s) + diff_y(tmp, 1)))
        for i, new in enumerate((new_p, new_q, new_s)):
            if t == TOP // 8 - 1:
                new = jnp.where(keep_low, new, 0.0)
            if t == TOP // 8 + 4:
                new = jnp.where(keep_high, new, 0.0)
            dst[i * cols : (i + 1) * cols, rows] = new


def run_steps(step, a, b):
    lo = TOP // 8
    step(a, b, lo - 2, lo + 6)
    step(b, a, lo - 2, lo + 6)
    step(a, b, lo - 2, lo + 6)

    def pair(_, carry):
        step(b, a, lo - 1, lo + 5)
        step(a, b, lo - 1, lo + 5)
        return carry

    lax.fori_loop(0, 4, pair, 0)
    step(b, a, lo, lo + 4)


def kernel(
    tms, strips, total_rows,
    inc_hbm, depth_hbm, wind_hbm, spread_hbm, decay_hbm, out_ref,
    raw, fa, fb, ref, tmp, fc, spread, decay,
    halo_out, halo_in, pre_out, pre_in, tan_out, tan_in, scan_b, w_own, w_in, wl_in, wh_in, wk_in, wk,
    load_sem, halo_send, halo_recv, pre_send, pre_recv, tan_send, tan_recv,
    w_send, w_recv, wh_send, wl_recv, wh_recv, wk_send, wk_recv,
):
    nine = fa.shape[0]
    cols = nine // 3
    rows = spread.shape[1]
    per = rows // tms
    halo = STEPS
    edge = halo // per
    tm = lax.axis_index("tm")
    strip = lax.axis_index("strip")
    has_low, has_high = strip > 0, strip < strips - 1
    to_low, to_high = jnp.logical_and(has_low, tm < edge), jnp.logical_and(has_high, tm >= tms - edge)

    barrier = pltpu.get_barrier_semaphore()

    @pl.when(has_low)
    def _():
        pl.semaphore_signal(barrier, inc=1, device_id=(tm, strip - 1), device_id_type=MESH)

    @pl.when(has_high)
    def _():
        pl.semaphore_signal(barrier, inc=1, device_id=(tm, strip + 1), device_id_type=MESH)

    for d in range(1, tms):
        pl.semaphore_signal(barrier, inc=1, device_id=(lax.rem(tm + d, tms), strip), device_id_type=MESH)

    loads = [
        pltpu.make_async_copy(hbm.at[0], buf, load_sem.at[n])
        for n, (hbm, buf) in enumerate((
            (inc_hbm, raw.at[0]), (depth_hbm, raw.at[1, 0:1]), (wind_hbm, raw.at[1, 1:3]),
            (spread_hbm, raw.at[2]), (decay_hbm, raw.at[3]),
        ))
    ]
    for copy in loads:
        copy.start()

    marks, into, back = column_maps(cols)
    own = pl.ds(TOP, rows)

    def regroup(n, p, buf, offset, scale):
        for t in range(rows // 8):
            at = pl.ds(8 * t, 8)
            parts = [raw[n, p, at, c * LANES : (c + 1) * LANES] for c in range(cols)]
            for j in range(cols):
                new = take_lanes(choose(marks, parts, j), into[j])
                buf[p * cols + j, pl.ds(offset + 8 * t, 8)] = new * scale if scale else new

    @pl.when(jnp.logical_not(has_low))
    def _():
        for buf in (fa, ref):
            buf[:, TOP - 16 : TOP] = jnp.zeros((nine, 16, LANES), jnp.float32)

    @pl.when(jnp.logical_not(has_high))
    def _():
        for buf in (fa, ref):
            buf[:, TOP + rows : TOP + rows + 16] = jnp.zeros((nine, 16, LANES), jnp.float32)

    row = lax.broadcasted_iota(jnp.int32, fc.shape, 0) + (strip * rows - TOP)
    fc[...] = DT * (0.2 + 0.4 * row.astype(jnp.float32) / total_rows)

    loads[0].wait()
    for p in range(3):
        regroup(0, p, fa, TOP, HALF if p == 0 else None)
    loads[1].wait()
    loads[2].wait()
    for p in range(3):
        regroup(1, p, ref, TOP, HALF * HALF if p == 0 else HALF)

    for i in range(nine):
        for n, buf in ((0, fa), (nine, ref)):
            at = (n + i) * halo
            halo_out[0, at : at + halo] = buf[i, TOP : TOP + halo]
            halo_out[1, at : at + halo] = buf[i, TOP + rows - halo : TOP + rows]

    inside = jnp.logical_and(has_low, has_high)

    @pl.when(inside)
    def _():
        pl.semaphore_wait(barrier, tms + 1)

    @pl.when(jnp.logical_not(inside))
    def _():
        pl.semaphore_wait(barrier, tms)

    to_below = pltpu.make_async_remote_copy(
        halo_out.at[0], halo_in.at[1], halo_send.at[0], halo_recv.at[1],
        device_id=(tm, strip - 1), device_id_type=MESH,
    )
    to_above = pltpu.make_async_remote_copy(
        halo_out.at[1], halo_in.at[0], halo_send.at[1], halo_recv.at[0],
        device_id=(tm, strip + 1), device_id_type=MESH,
    )

    @pl.when(has_low)
    def _():
        to_below.start()

    @pl.when(has_high)
    def _():
        to_above.start()

    def wait_for(slabs, sem):
        pltpu.make_async_copy(slabs, slabs, sem).wait()

    def spread_out(out, into, send, recv):
        copies = []
        for d in range(1, tms):
            to = lax.rem(tm + d, tms)
            copies.append(pltpu.make_async_remote_copy(
                out.at[to], into.at[tm], send, recv,
                device_id=(to, strip), device_id_type=MESH,
            ))
        for copy in copies:
            copy.start()
        into[tm] = out[tm]

    for n, buf in ((2, spread), (3, decay)):
        loads[n + 1].wait()
        for p in range(3):
            regroup(n, p, buf, 0, None)
    for i in range(nine):
        for j in range(tms):
            here = slice(per * j, per * (j + 1))
            for n, part in enumerate((fa[i, TOP + per * j : TOP + per * (j + 1)], spread[i, here], decay[i, here])):
                at = per * (n * nine + i)
                pre_out[j, at : at + per] = part
    spread_out(pre_out, pre_in, pre_send, pre_recv)

    @pl.when(has_low)
    def _():
        to_above.wait_recv()
        for i in range(nine):
            for n, buf in ((0, fa), (nine, ref)):
                buf[i, TOP - halo : TOP] = halo_in[0, (n + i) * halo : (n + i + 1) * halo]

    @pl.when(has_high)
    def _():
        to_below.wait_recv()
        for i in range(nine):
            for n, buf in ((0, fa), (nine, ref)):
                buf[i, TOP + rows : TOP + rows + halo] = halo_in[1, (n + i) * halo : (n + i + 1) * halo]

    run_steps(
        lambda a, b, first, stop: tangent_step(a, b, ref, tmp, fc, first, stop, has_low, has_high), fa, fb
    )
    for i in range(nine):
        for j in range(tms):
            tan_out[j, per * i : per * (i + 1)] = fa[i, TOP + per * j : TOP + per * (j + 1)]

    spread_out(tan_out, tan_in, tan_send, tan_recv)

    others = pl.ds(0, tms - 1)
    wait_for(pre_in.at[others], pre_recv)
    wait_for(tan_in.at[others], tan_recv)
    flat = per * nine
    built = None
    for k in range(tms):
        residual = pre_in[k, 0:flat]
        if k:
            residual = residual - tan_in[k - 1]
        scaled = pre_in[k, flat : 2 * flat] * residual
        built = scaled if k == 0 else pre_in[k, 2 * flat :] * built + scaled
        scan_b[k] = built
    w_own[tms] = jnp.zeros((flat, LANES), jnp.float32)
    smoothed = None
    for k in reversed(range(tms)):
        smoothed = scan_b[k] if smoothed is None else scan_b[k] + pre_in[k + 1, 2 * flat :] * smoothed
        w_own[k] = pre_in[k, flat : 2 * flat] * smoothed

    w_copies, low_copies, high_copies, wk_copies = [], [], [], []
    for d in range(tms):
        to = lax.rem(tm + d, tms)
        low_copies.append(pltpu.make_async_remote_copy(
            w_own.at[to + 1], wh_in.at[lax.rem(tm, edge)], wh_send, wh_recv,
            device_id=(to, strip - 1), device_id_type=MESH,
        ))
        high_copies.append(pltpu.make_async_remote_copy(
            w_own.at[to + 1], wl_in.at[lax.rem(tm + edge - (tms - edge) % edge, edge)], wh_send, wl_recv,
            device_id=(to, strip + 1), device_id_type=MESH,
        ))
        if d:
            w_copies.append(pltpu.make_async_remote_copy(
                w_own.at[to + 1], w_in.at[tm], w_send, w_recv,
                device_id=(to, strip), device_id_type=MESH,
            ))
            wk_copies.append(pltpu.make_async_remote_copy(
                w_own.at[to], wk_in.at[tm], wk_send, wk_recv,
                device_id=(to, strip), device_id_type=MESH,
            ))

    @pl.when(to_low)
    def _():
        for copy in low_copies:
            copy.start()

    @pl.when(to_high)
    def _():
        for copy in high_copies:
            copy.start()

    for copy in w_copies:
        copy.start()
    for copy in wk_copies:
        copy.start()
    w_in[tm] = w_own[tm + 1]
    wk_in[tm] = w_own[tm]

    @pl.when(jnp.logical_not(has_low))
    def _():
        fa[:, TOP - 16 : TOP] = jnp.zeros((nine, 16, LANES), jnp.float32)

    @pl.when(jnp.logical_not(has_high))
    def _():
        fa[:, TOP + rows : TOP + rows + 16] = jnp.zeros((nine, 16, LANES), jnp.float32)

    def unpack(slab, at):
        for i in range(nine):
            part = slab[per * i : per * (i + 1)]
            fa[i, at : at + per] = part * (1.0 / HALF**2) if i < cols else part

    wait_for(w_in.at[others], w_recv)
    for j in range(tms):
        unpack(w_in.at[j], TOP + per * j)

    @pl.when(has_low)
    def _():
        wait_for(wl_in, wl_recv)
        for q in range(edge):
            unpack(wl_in.at[q], TOP - halo + per * q)

    @pl.when(has_high)
    def _():
        wait_for(wh_in, wh_recv)
        for q in range(edge):
            unpack(wh_in.at[q], TOP + rows + per * q)

    run_steps(
        lambda a, b, first, stop: adjoint_step(a, b, ref, tmp, fc, first, stop, has_low, has_high), fa, fb
    )
    wait_for(wk_in.at[others], wk_recv)
    for j in range(tms):
        for i in range(nine):
            wk[i, per * j : per * (j + 1)] = wk_in[j, per * i : per * (i + 1)]
    for p in range(3):
        for t in range(rows // 8):
            at = pl.ds(8 * t, 8)
            parts = []
            for j in range(cols):
                weighted, adjoint = wk[p * cols + j, at], fa[p * cols + j, pl.ds(TOP + 8 * t, 8)]
                if p == 0:
                    weighted, adjoint = weighted * (1.0 / HALF), adjoint * HALF
                parts.append(take_lanes(weighted - adjoint, back[j]))
            for c in range(cols):
                out_ref[0, p, at, c * LANES : (c + 1) * LANES] = choose(marks, parts, c)

    @pl.when(has_low)
    def _():
        to_below.wait_send()

    @pl.when(has_high)
    def _():
        to_above.wait_send()

    @pl.when(jnp.logical_or(to_low, to_high))
    def _():
        wait_for(w_own.at[pl.ds(0, tms)], wh_send)

    for slabs, sem in ((pre_out, pre_send), (tan_out, tan_send), (w_own, w_send), (w_own, wk_send)):
        wait_for(slabs.at[others], sem)


def body(tms, strips, increment, ref_depth, ref_wind, spread, decay):
    _, planes, rows, width = increment.shape
    cols = width // LANES
    nine = planes * cols
    per = rows // tms
    flat = per * nine
    edge = STEPS // per
    height = rows + 2 * TOP
    dma = pltpu.SemaphoreType.DMA
    f32 = jnp.float32
    vmem = lambda *shape: pltpu.VMEM(shape, f32)
    hbm = pl.BlockSpec(memory_space=pl.ANY)
    return pl.pallas_call(
        functools.partial(kernel, tms, strips, strips * rows),
        out_shape=jax.ShapeDtypeStruct(increment.shape, f32),
        in_specs=[hbm] * 5,
        out_specs=pl.BlockSpec(memory_space=pltpu.VMEM),
        scratch_shapes=[
            vmem(4, planes, rows, width),
            vmem(nine, height, LANES), vmem(nine, height, LANES), vmem(nine, height, LANES),
            vmem(2 * cols, height, LANES), vmem(height, LANES),
            vmem(nine, rows, LANES), vmem(nine, rows, LANES),
            vmem(2, 2 * nine * STEPS, LANES), vmem(2, 2 * nine * STEPS, LANES),
            vmem(tms, 3 * flat, LANES), vmem(tms, 3 * flat, LANES),
            vmem(tms, flat, LANES), vmem(tms, flat, LANES),
            vmem(tms, flat, LANES), vmem(tms + 1, flat, LANES), vmem(tms, flat, LANES),
            vmem(edge, flat, LANES), vmem(edge, flat, LANES), vmem(tms, flat, LANES),
            vmem(nine, rows, LANES),
            dma((5,)), dma((2,)), dma((2,)), *[dma] * 11,
        ],
        compiler_params=pltpu.CompilerParams(
            collective_id=0, has_side_effects=True, vmem_limit_bytes=24 * 2**20
        ),
    )(*(pltpu.with_memory_space_constraint(x, pltpu.HBM) for x in (increment, ref_depth, ref_wind, spread, decay)))


def solution(mesh):
    spec = P("tm", None, "strip", None)
    return jax.shard_map(
        functools.partial(body, mesh.shape["tm"], mesh.shape["strip"]),
        mesh=mesh,
        in_specs=(spec,) * 5,
        out_specs=spec,
        check_vma=False,
    )
```

```python
import functools

import jax
import jax.numpy as jnp
from jax import lax
from jax.experimental import pallas as pl
from jax.experimental.pallas import tpu as pltpu
from jax.sharding import PartitionSpec as P

STEPS = 12
DT = 0.4
HALF = 0.5 * DT
LANES = 128
TOP = 24
MESH = pl.DeviceIdType.MESH
ORDER = [(dy, dx, dc) for dx in (0, 1) for dy in (2, 1, 3, 0) for dc in (0, 1)]
NEAR, FAR = ORDER[:8], ORDER[8:]
RETURN = ((FAR, NEAR), (NEAR, FAR))


def diff_x(f):
    after = pltpu.roll(f[:1], LANES - 1, 2)
    before = pltpu.roll(f[-1:], 1, 2)
    return jnp.concatenate([f[1:], after], axis=0) - jnp.concatenate([before, f[:-1]], axis=0)


def third(x):
    return (x * 21846) >> 16


def column_maps(cols):
    lane = lax.broadcasted_iota(jnp.int32, (8, LANES), 1)
    rest = lane - cols * third(lane)
    into, back = [], []
    for j in range(cols):
        x = cols * lane + j
        into.append(x & (LANES - 1))
        block = rest + 2 * j
        block = block - cols * third(block)
        back.append(third(LANES * block + lane - j))
    return (rest == 0, rest == 1), into, back


def choose(marks, parts, j):
    pick = [parts[(2 * j + r) % len(parts)] for r in range(3)]
    return jnp.where(marks[0], pick[0], jnp.where(marks[1], pick[1], pick[2]))


def take_lanes(x, index):
    return jnp.take_along_axis(x, index, axis=1, mode="promise_in_bounds")


def tangent_products(new, ref, rows, tmp):
    cols = tmp.shape[0] // 2
    tmp[:cols, rows] = ref[0:cols, rows] * new[2] + ref[2 * cols :, rows] * new[0]


def tangent_tile(src, ref, tmp, fc, at):
    cols = src.shape[0] // 3
    rows, below, above = (pl.ds(at + d, 8) for d in (0, -1, 1))

    def diff_y(buf, i):
        return buf[i * cols : (i + 1) * cols, above] - buf[i * cols : (i + 1) * cols, below]

    h, u, v = (src[i * cols : (i + 1) * cols, rows] for i in range(3))
    depth, east, north = (ref[i * cols : (i + 1) * cols, rows] for i in range(3))
    turn = fc[rows][None]
    flux = depth * u + east * h
    new_h = h - (diff_x(flux) + diff_y(tmp, 0))
    new_u = u - ((east * diff_x(u) + north * diff_y(src, 1)) + (diff_x(h) - turn * v))
    new_v = v - ((east * diff_x(v) + north * diff_y(src, 2)) + (diff_y(src, 0) + turn * u))
    return new_h, new_u, new_v


def adjoint_products(new, ref, rows, tmp):
    cols = tmp.shape[0] // 2
    north = ref[2 * cols :, rows]
    tmp[:cols, rows] = north * new[1]
    tmp[cols:, rows] = north * new[2]


def adjoint_tile(src, ref, tmp, fc, at):
    cols = src.shape[0] // 3
    rows, below, above = (pl.ds(at + d, 8) for d in (0, -1, 1))

    def diff_y(buf, i):
        return buf[i * cols : (i + 1) * cols, above] - buf[i * cols : (i + 1) * cols, below]

    p, q, s = (src[i * cols : (i + 1) * cols, rows] for i in range(3))
    depth, east, north = (ref[i * cols : (i + 1) * cols, rows] for i in range(3))
    turn = fc[rows][None]
    px, py = diff_x(p), diff_y(src, 0)
    new_p = p + ((east * px + north * py) + (diff_x(q) + diff_y(src, 2)))
    new_q = q + ((depth * px - turn * s) + (diff_x(east * q) + diff_y(tmp, 0)))
    new_s = s + ((depth * py + turn * q) + (diff_x(east * s) + diff_y(tmp, 1)))
    return new_p, new_q, new_s


def run_steps(tile, products, bufs, ref, fc, rows, has_low, has_high):
    lo, hi = TOP // 8, (TOP + rows) // 8
    cols = ref.shape[0] // 3

    for t in range(lo - 2, hi + 2):
        at = pl.ds(8 * t, 8)
        products([bufs[0][0][i * cols : (i + 1) * cols, at] for i in range(3)], ref, at, bufs[0][1])

    def step(j, more, last=False):
        (src, tmp), (dst, new_tmp) = bufs if j % 2 else bufs[::-1]
        for t in range(lo - more, hi + more):
            new = tile(src, ref, tmp, fc, 8 * t)
            if t == lo - 1:
                new = [jnp.where(has_low, x, 0.0) for x in new]
            if t == hi:
                new = [jnp.where(has_high, x, 0.0) for x in new]
            at = pl.ds(8 * t, 8)
            for i, x in enumerate(new):
                dst[i * cols : (i + 1) * cols, at] = x
            if not last:
                products(new, ref, at, new_tmp)

    for j in (1, 2, 3):
        step(j, 2)

    def pair(_, carry):
        for j in (4, 5, 6, 7):
            step(j, 1)
        return carry

    lax.fori_loop(0, 2, pair, 0)
    step(STEPS, 0, last=True)


def kernel(
    tms, strips, total_rows,
    inc_hbm, depth_hbm, wind_hbm, spread_hbm, decay_hbm, out_ref,
    raw, fa, fb, ref, tmp_a, tmp_b, fc, spread, decay,
    halo_out, halo_in, pre_out, pre_in, inc_out, inc_in, mate, tan_out, tan_in, scan_b, w_own, w_in, wl_in, wh_in, wk_in, wk,
    load_sem, halo_send, halo_recv, pre_send, pre_recv, inc_send, inc_recv, mate_send, mate_recv, tan_send, tan_recv,
    w_send, w_recv, wh_send, wl_recv, wh_recv, wk_send, wk_recv,
):
    nine = fa.shape[0]
    cols = nine // 3
    rows = spread.shape[1]
    per = rows // tms
    flat = per * nine
    bufs = ((fa, tmp_a), (fb, tmp_b))
    halo = STEPS
    edge = halo // per
    tm = lax.axis_index("tm")
    strip = lax.axis_index("strip")
    has_low, has_high = strip > 0, strip < strips - 1
    even, odd = lax.rem(tm, 2) == 0, lax.rem(tm, 2) == 1
    to_low, to_high = jnp.logical_and(has_low, tm < edge), jnp.logical_and(has_high, tm >= tms - edge)

    def partner(dy, dx, dc):
        y, x, c = lax.div(tm, 4), lax.rem(lax.div(tm, 2), 2), lax.rem(tm, 2)
        return 4 * lax.rem(y + dy, tms // 4) + 2 * (1 - x if dx else x) + (1 - c if dc else c)

    def others_by(order):
        return [partner(*way) for way in order if way != (0, 0, 0)]

    barrier = pltpu.get_barrier_semaphore()

    @pl.when(has_low)
    def _():
        pl.semaphore_signal(barrier, inc=1, device_id=(tm, strip - 1), device_id_type=MESH)

    @pl.when(has_high)
    def _():
        pl.semaphore_signal(barrier, inc=1, device_id=(tm, strip + 1), device_id_type=MESH)

    for d in range(1, tms):
        pl.semaphore_signal(barrier, inc=1, device_id=(lax.rem(tm + d, tms), strip), device_id_type=MESH)

    loads = [
        pltpu.make_async_copy(hbm.at[0], buf, load_sem.at[n])
        for n, (hbm, buf) in enumerate((
            (inc_hbm, raw.at[0]), (depth_hbm, raw.at[1, 0:1]), (wind_hbm, raw.at[1, 1:3]),
            (spread_hbm, raw.at[2]), (decay_hbm, raw.at[3]),
        ))
    ]
    for copy in loads:
        copy.start()

    marks, into, back = column_maps(cols)
    own = pl.ds(TOP, rows)

    def regroup(n, p, buf, offset, scale):
        for t in range(rows // 8):
            at = pl.ds(8 * t, 8)
            parts = [raw[n, p, at, c * LANES : (c + 1) * LANES] for c in range(cols)]
            for j in range(cols):
                new = take_lanes(choose(marks, parts, j), into[j])
                buf[p * cols + j, pl.ds(offset + 8 * t, 8)] = new * scale if scale else new

    @pl.when(jnp.logical_not(has_low))
    def _():
        for buf in (fa, ref):
            buf[:, TOP - 16 : TOP] = jnp.zeros((nine, 16, LANES), jnp.float32)

    @pl.when(jnp.logical_not(has_high))
    def _():
        for buf in (fa, ref):
            buf[:, TOP + rows : TOP + rows + 16] = jnp.zeros((nine, 16, LANES), jnp.float32)

    row = lax.broadcasted_iota(jnp.int32, fc.shape, 0) + (strip * rows - TOP)
    fc[...] = DT * (0.2 + 0.4 * row.astype(jnp.float32) / total_rows)

    loads[0].wait()
    for p in range(3):
        regroup(0, p, fa, TOP, HALF if p == 0 else None)
    loads[1].wait()
    loads[2].wait()
    for p in range(3):
        regroup(1, p, ref, TOP, HALF * HALF if p == 0 else HALF)

    for i in range(nine):
        for n, buf in ((0, fa), (nine, ref)):
            at = (n + i) * halo
            halo_out[0, at : at + halo] = buf[i, TOP : TOP + halo]
            halo_out[1, at : at + halo] = buf[i, TOP + rows - halo : TOP + rows]

    inside = jnp.logical_and(has_low, has_high)

    @pl.when(inside)
    def _():
        pl.semaphore_wait(barrier, tms + 1)

    @pl.when(jnp.logical_not(inside))
    def _():
        pl.semaphore_wait(barrier, tms)

    to_below = pltpu.make_async_remote_copy(
        halo_out.at[0], halo_in.at[1], halo_send.at[0], halo_recv.at[1],
        device_id=(tm, strip - 1), device_id_type=MESH,
    )
    to_above = pltpu.make_async_remote_copy(
        halo_out.at[1], halo_in.at[0], halo_send.at[1], halo_recv.at[0],
        device_id=(tm, strip + 1), device_id_type=MESH,
    )

    across_above = lax.rem(strip, 2) == 0

    @pl.when(jnp.logical_and(has_low, across_above))
    def _():
        to_below.start()

    @pl.when(has_high)
    def _():
        to_above.start()

    @pl.when(jnp.logical_and(has_low, jnp.logical_not(across_above)))
    def _():
        to_below.start()

    def wait_for(slabs, sem):
        pltpu.make_async_copy(slabs, slabs, sem).wait()

    def spread_out(out, into, send, recv):
        copies = []
        for to in others_by(ORDER):
            copies.append(pltpu.make_async_remote_copy(
                out.at[to], into.at[tm], send, recv,
                device_id=(to, strip), device_id_type=MESH,
            ))
        for copy in copies:
            copy.start()
        into[tm] = out[tm]

    for n, buf in ((2, spread), (3, decay)):
        loads[n + 1].wait()
        for p in range(3):
            regroup(n, p, buf, 0, None)
    for i in range(nine):
        for j in range(tms):
            here = slice(per * j, per * (j + 1))
            inc_out[j, per * i : per * (i + 1)] = fa[i, TOP + per * j : TOP + per * (j + 1)]
            pre_out[j, per * i : per * (i + 1)] = spread[i, here]
            pre_out[j, flat + per * i : flat + per * (i + 1)] = decay[i, here]
    to_mate = pltpu.make_async_remote_copy(
        inc_out, mate, mate_send, mate_recv, device_id=(jnp.maximum(tm - 1, 0), strip), device_id_type=MESH
    )

    @pl.when(odd)
    def _():
        to_mate.start()
        mate[...] = jnp.zeros_like(mate)

    @pl.when(even)
    def _():
        spread_out(inc_out, inc_in, inc_send, inc_recv)

    spread_out(pre_out, pre_in, pre_send, pre_recv)

    @pl.when(has_low)
    def _():
        to_above.wait_recv()
        for i in range(nine):
            for n, buf in ((0, fa), (nine, ref)):
                buf[i, TOP - halo : TOP] = halo_in[0, (n + i) * halo : (n + i + 1) * halo]

    @pl.when(has_high)
    def _():
        to_below.wait_recv()
        for i in range(nine):
            for n, buf in ((0, fa), (nine, ref)):
                buf[i, TOP + rows : TOP + rows + halo] = halo_in[1, (n + i) * halo : (n + i + 1) * halo]

    run_steps(tangent_tile, tangent_products, bufs, ref, fc, rows, has_low, has_high)
    @pl.when(even)
    def _():
        to_mate.wait_recv()

    for i in range(nine):
        for j in range(tms):
            at = slice(per * i, per * (i + 1))
            tan_out[j, at] = mate[j, at] - fa[i, TOP + per * j : TOP + per * (j + 1)]

    spread_out(tan_out, tan_in, tan_send, tan_recv)

    others = pl.ds(0, tms - 1)
    wait_for(pre_in.at[others], pre_recv)

    @pl.when(even)
    def _():
        wait_for(inc_in.at[pl.ds(0, tms // 2 - 1)], inc_recv)

    @pl.when(odd)
    def _():
        wait_for(inc_in.at[pl.ds(0, tms // 2)], inc_recv)

    wait_for(tan_in.at[others], tan_recv)
    built = None
    for k in range(tms):
        residual = inc_in[k] if k == 0 else tan_in[k - 1] if k % 2 else inc_in[k] + tan_in[k - 1]
        scaled = pre_in[k, 0:flat] * residual
        built = scaled if k == 0 else pre_in[k, flat:] * built + scaled
        scan_b[k] = built
    w_own[tms] = jnp.zeros((flat, LANES), jnp.float32)
    smoothed = None
    for k in reversed(range(tms)):
        smoothed = scan_b[k] if smoothed is None else scan_b[k] + pre_in[k + 1, flat:] * smoothed
        w_own[k] = pre_in[k, 0:flat] * smoothed

    def to_low_halo(to):
        return pltpu.make_async_remote_copy(
            w_own.at[to + 1], wh_in.at[lax.rem(tm, edge)], wh_send, wh_recv,
            device_id=(to, strip - 1), device_id_type=MESH,
        )

    def to_high_halo(to):
        at = lax.rem(tm + edge - (tms - edge) % edge, edge)
        return pltpu.make_async_remote_copy(
            w_own.at[to + 1], wl_in.at[at], wh_send, wl_recv,
            device_id=(to, strip + 1), device_id_type=MESH,
        )

    def to_same(to, shift, into, send, recv):
        return pltpu.make_async_remote_copy(
            w_own.at[to + shift], into.at[tm], send, recv, device_id=(to, strip), device_id_type=MESH
        )

    for ways, halo_ways in RETURN:
        @pl.when(to_low)
        def _():
            for way in halo_ways:
                to_low_halo(partner(*way)).start()

        @pl.when(to_high)
        def _():
            for way in halo_ways:
                to_high_halo(partner(*way)).start()

        for to in others_by(ways):
            to_same(to, 1, w_in, w_send, w_recv).start()
    for to in others_by(ORDER):
        to_same(to, 0, wk_in, wk_send, wk_recv).start()
    w_in[tm] = w_own[tm + 1]
    wk_in[tm] = w_own[tm]

    @pl.when(jnp.logical_not(has_low))
    def _():
        fa[:, TOP - 16 : TOP] = jnp.zeros((nine, 16, LANES), jnp.float32)

    @pl.when(jnp.logical_not(has_high))
    def _():
        fa[:, TOP + rows : TOP + rows + 16] = jnp.zeros((nine, 16, LANES), jnp.float32)

    def unpack(slab, at):
        for i in range(nine):
            part = slab[per * i : per * (i + 1)]
            fa[i, at : at + per] = part * (1.0 / HALF**2) if i < cols else part

    wait_for(w_in.at[others], w_recv)
    for j in range(tms):
        unpack(w_in.at[j], TOP + per * j)

    @pl.when(has_low)
    def _():
        wait_for(wl_in, wl_recv)
        for q in range(edge):
            unpack(wl_in.at[q], TOP - halo + per * q)

    @pl.when(has_high)
    def _():
        wait_for(wh_in, wh_recv)
        for q in range(edge):
            unpack(wh_in.at[q], TOP + rows + per * q)

    run_steps(adjoint_tile, adjoint_products, bufs, ref, fc, rows, has_low, has_high)
    wait_for(wk_in.at[others], wk_recv)
    for j in range(tms):
        for i in range(nine):
            wk[i, per * j : per * (j + 1)] = wk_in[j, per * i : per * (i + 1)]
    for p in range(3):
        for t in range(rows // 8):
            at = pl.ds(8 * t, 8)
            parts = []
            for j in range(cols):
                weighted, adjoint = wk[p * cols + j, at], fa[p * cols + j, pl.ds(TOP + 8 * t, 8)]
                if p == 0:
                    weighted, adjoint = weighted * (1.0 / HALF), adjoint * HALF
                parts.append(take_lanes(weighted - adjoint, back[j]))
            for c in range(cols):
                out_ref[0, p, at, c * LANES : (c + 1) * LANES] = choose(marks, parts, c)

    @pl.when(has_low)
    def _():
        to_below.wait_send()

    @pl.when(has_high)
    def _():
        to_above.wait_send()

    @pl.when(jnp.logical_or(to_low, to_high))
    def _():
        wait_for(w_own.at[pl.ds(0, tms)], wh_send)

    @pl.when(even)
    def _():
        wait_for(inc_out.at[others], inc_send)

    @pl.when(odd)
    def _():
        to_mate.wait_send()

    for slabs, sem in ((pre_out, pre_send), (tan_out, tan_send), (w_own, w_send), (w_own, wk_send)):
        wait_for(slabs.at[others], sem)


def body(tms, strips, increment, ref_depth, ref_wind, spread, decay):
    _, planes, rows, width = increment.shape
    cols = width // LANES
    nine = planes * cols
    per = rows // tms
    flat = per * nine
    edge = STEPS // per
    height = rows + 2 * TOP
    dma = pltpu.SemaphoreType.DMA
    f32 = jnp.float32
    vmem = lambda *shape: pltpu.VMEM(shape, f32)
    hbm = pl.BlockSpec(memory_space=pl.ANY)
    return pl.pallas_call(
        functools.partial(kernel, tms, strips, strips * rows),
        out_shape=jax.ShapeDtypeStruct(increment.shape, f32),
        in_specs=[hbm] * 5,
        out_specs=pl.BlockSpec(memory_space=pltpu.VMEM),
        scratch_shapes=[
            vmem(4, planes, rows, width),
            vmem(nine, height, LANES), vmem(nine, height, LANES), vmem(nine, height, LANES),
            vmem(2 * cols, height, LANES), vmem(2 * cols, height, LANES), vmem(height, LANES),
            vmem(nine, rows, LANES), vmem(nine, rows, LANES),
            vmem(2, 2 * nine * STEPS, LANES), vmem(2, 2 * nine * STEPS, LANES),
            vmem(tms, 2 * flat, LANES), vmem(tms, 2 * flat, LANES),
            vmem(tms, flat, LANES), vmem(tms, flat, LANES), vmem(tms, flat, LANES),
            vmem(tms, flat, LANES), vmem(tms, flat, LANES),
            vmem(tms, flat, LANES), vmem(tms + 1, flat, LANES), vmem(tms, flat, LANES),
            vmem(edge, flat, LANES), vmem(edge, flat, LANES), vmem(tms, flat, LANES),
            vmem(nine, rows, LANES),
            dma((5,)), dma((2,)), dma((2,)), *[dma] * 15,
        ],
        compiler_params=pltpu.CompilerParams(
            collective_id=0, has_side_effects=True, vmem_limit_bytes=24 * 2**20
        ),
    )(*(pltpu.with_memory_space_constraint(x, pltpu.HBM) for x in (increment, ref_depth, ref_wind, spread, decay)))


def solution(mesh):
    spec = P("tm", None, "strip", None)
    return jax.shard_map(
        functools.partial(body, mesh.shape["tm"], mesh.shape["strip"]),
        mesh=mesh,
        in_specs=(spec,) * 5,
        out_specs=spec,
        check_vma=False,
    )
```

```python
import functools

import jax
import jax.numpy as jnp
from jax import lax
from jax.experimental import pallas as pl
from jax.experimental.pallas import tpu as pltpu
from jax.sharding import PartitionSpec as P

STEPS = 12
DT = 0.4
HALF = 0.5 * DT
LANES = 128
TOP = 24
MESH = pl.DeviceIdType.MESH
ORDER = [(dy, dx, dc) for dx in (0, 1) for dy in (2, 1, 3, 0) for dc in (0, 1)]
NEAR, FAR = ORDER[:8], ORDER[8:]
RETURN = ((FAR, NEAR), (NEAR, FAR))


def diff_x(f):
    after = pltpu.roll(f[:1], LANES - 1, 2)
    before = pltpu.roll(f[-1:], 1, 2)
    return jnp.concatenate([f[1:], after], axis=0) - jnp.concatenate([before, f[:-1]], axis=0)


def third(x):
    return (x * 21846) >> 16


def column_maps(cols):
    lane = lax.broadcasted_iota(jnp.int32, (8, LANES), 1)
    rest = lane - cols * third(lane)
    into, back = [], []
    for j in range(cols):
        x = cols * lane + j
        into.append(x & (LANES - 1))
        block = rest + 2 * j
        block = block - cols * third(block)
        back.append(third(LANES * block + lane - j))
    return (rest == 0, rest == 1), into, back


def choose(marks, parts, j):
    pick = [parts[(2 * j + r) % len(parts)] for r in range(3)]
    return jnp.where(marks[0], pick[0], jnp.where(marks[1], pick[1], pick[2]))


def take_lanes(x, index):
    return jnp.take_along_axis(x, index, axis=1, mode="promise_in_bounds")


def tangent_products(new, ref, rows, tmp):
    cols = tmp.shape[0] // 2
    tmp[:cols, rows] = ref[0:cols, rows] * new[2] + ref[2 * cols :, rows] * new[0]


def tangent_tile(src, ref, tmp, fc, at):
    cols = src.shape[0] // 3
    rows, below, above = (pl.ds(at + d, 8) for d in (0, -1, 1))

    def diff_y(buf, i):
        return buf[i * cols : (i + 1) * cols, above] - buf[i * cols : (i + 1) * cols, below]

    h, u, v = (src[i * cols : (i + 1) * cols, rows] for i in range(3))
    depth, east, north = (ref[i * cols : (i + 1) * cols, rows] for i in range(3))
    turn = fc[rows][None]
    flux = depth * u + east * h
    new_h = h - (diff_x(flux) + diff_y(tmp, 0))
    new_u = u - ((east * diff_x(u) + north * diff_y(src, 1)) + (diff_x(h) - turn * v))
    new_v = v - ((east * diff_x(v) + north * diff_y(src, 2)) + (diff_y(src, 0) + turn * u))
    return new_h, new_u, new_v


def adjoint_products(new, ref, rows, tmp):
    cols = tmp.shape[0] // 2
    north = ref[2 * cols :, rows]
    tmp[:cols, rows] = north * new[1]
    tmp[cols:, rows] = north * new[2]


def adjoint_tile(src, ref, tmp, fc, at):
    cols = src.shape[0] // 3
    rows, below, above = (pl.ds(at + d, 8) for d in (0, -1, 1))

    def diff_y(buf, i):
        return buf[i * cols : (i + 1) * cols, above] - buf[i * cols : (i + 1) * cols, below]

    p, q, s = (src[i * cols : (i + 1) * cols, rows] for i in range(3))
    depth, east, north = (ref[i * cols : (i + 1) * cols, rows] for i in range(3))
    turn = fc[rows][None]
    px, py = diff_x(p), diff_y(src, 0)
    new_p = p + ((east * px + north * py) + (diff_x(q) + diff_y(src, 2)))
    new_q = q + ((depth * px - turn * s) + (diff_x(east * q) + diff_y(tmp, 0)))
    new_s = s + ((depth * py + turn * q) + (diff_x(east * s) + diff_y(tmp, 1)))
    return new_p, new_q, new_s


def run_steps(tile, products, bufs, ref, fc, rows, has_low, has_high, spreads):
    lo, hi = TOP // 8, (TOP + rows) // 8
    cols = ref.shape[0] // 3

    reach = 1 if spreads else 2
    for t in range(lo - reach, hi + reach):
        at = pl.ds(8 * t, 8)
        products([bufs[0][0][i * cols : (i + 1) * cols, at] for i in range(3)], ref, at, bufs[0][1])

    def step(j, more, last=False):
        (src, tmp), (dst, new_tmp) = bufs if j % 2 else bufs[::-1]
        for t in range(lo - more, hi + more):
            new = tile(src, ref, tmp, fc, 8 * t)
            if t == lo - 1:
                new = [jnp.where(has_low, x, 0.0) for x in new]
            if t == hi:
                new = [jnp.where(has_high, x, 0.0) for x in new]
            at = pl.ds(8 * t, 8)
            for i, x in enumerate(new):
                dst[i * cols : (i + 1) * cols, at] = x
            if not last:
                products(new, ref, at, new_tmp)

    def four(first):
        def turn(_, carry):
            for j in range(first, first + 4):
                step(j, 1)
            return carry

        lax.fori_loop(0, 2, turn, 0)

    if spreads:
        four(1)
        for j in range(9, STEPS + 1):
            step(j, 2, last=j == STEPS)
    else:
        for j in (1, 2, 3):
            step(j, 2)
        four(4)
        step(STEPS, 0, last=True)


def kernel(
    tms, strips, total_rows,
    inc_hbm, depth_hbm, wind_hbm, spread_hbm, decay_hbm, out_ref,
    raw, fa, fb, ref, tmp_a, tmp_b, fc, spread, decay,
    halo_out, halo_in, pre_out, pre_in, inc_out, inc_in, mate, tan_out, tan_in, beside_out, beside_in, scan_b, w_own, w_in, wl_in, wh_in, wk_in, wk,
    load_sem, halo_send, halo_recv, pre_send, pre_recv, inc_send, inc_recv, mate_send, mate_recv, tan_send, tan_recv, beside_send, beside_recv,
    w_send, w_recv, wh_send, wl_recv, wh_recv, wk_send, wk_recv,
):
    nine = fa.shape[0]
    cols = nine // 3
    rows = spread.shape[1]
    per = rows // tms
    flat = per * nine
    bufs = ((fa, tmp_a), (fb, tmp_b))
    halo = STEPS
    edge = halo // per
    tm = lax.axis_index("tm")
    strip = lax.axis_index("strip")
    has_low, has_high = strip > 0, strip < strips - 1
    even, odd = lax.rem(tm, 2) == 0, lax.rem(tm, 2) == 1
    to_low, to_high = jnp.logical_and(has_low, tm < edge), jnp.logical_and(has_high, tm >= tms - edge)

    def partner(dy, dx, dc):
        y, x, c = lax.div(tm, 4), lax.rem(lax.div(tm, 2), 2), lax.rem(tm, 2)
        return 4 * lax.rem(y + dy, tms // 4) + 2 * (1 - x if dx else x) + (1 - c if dc else c)

    def others_by(order):
        return [partner(*way) for way in order if way != (0, 0, 0)]

    barrier = pltpu.get_barrier_semaphore()

    @pl.when(has_low)
    def _():
        pl.semaphore_signal(barrier, inc=1, device_id=(tm, strip - 1), device_id_type=MESH)

    @pl.when(has_high)
    def _():
        pl.semaphore_signal(barrier, inc=1, device_id=(tm, strip + 1), device_id_type=MESH)

    for d in range(1, tms):
        pl.semaphore_signal(barrier, inc=1, device_id=(lax.rem(tm + d, tms), strip), device_id_type=MESH)

    loads = [
        pltpu.make_async_copy(hbm.at[0], buf, load_sem.at[n])
        for n, (hbm, buf) in enumerate((
            (inc_hbm, raw.at[0]), (depth_hbm, raw.at[1, 0:1]), (wind_hbm, raw.at[1, 1:3]),
            (spread_hbm, raw.at[2]), (decay_hbm, raw.at[3]),
        ))
    ]
    for copy in loads:
        copy.start()

    marks, into, back = column_maps(cols)
    own = pl.ds(TOP, rows)

    def regroup(n, p, buf, offset, scale):
        for t in range(rows // 8):
            at = pl.ds(8 * t, 8)
            parts = [raw[n, p, at, c * LANES : (c + 1) * LANES] for c in range(cols)]
            for j in range(cols):
                new = take_lanes(choose(marks, parts, j), into[j])
                buf[p * cols + j, pl.ds(offset + 8 * t, 8)] = new * scale if scale else new

    for buf in (fa, fb, ref, tmp_a, tmp_b):
        nothing = jnp.zeros((buf.shape[0], 16, LANES), jnp.float32)
        buf[:, TOP - 16 : TOP] = nothing
        buf[:, TOP + rows : TOP + rows + 16] = nothing

    @pl.when(jnp.logical_not(jnp.logical_or(to_low, to_high)))
    def _():
        beside_in[...] = jnp.zeros_like(beside_in)

    row = lax.broadcasted_iota(jnp.int32, fc.shape, 0) + (strip * rows - TOP)
    fc[...] = DT * (0.2 + 0.4 * row.astype(jnp.float32) / total_rows)

    loads[1].wait()
    loads[2].wait()
    for p in range(3):
        regroup(1, p, ref, TOP, HALF * HALF if p == 0 else HALF)
    rest = halo_out.shape[1] - nine * halo
    halo_out[:, nine * halo :] = jnp.zeros((2, rest, LANES), jnp.float32)
    for i in range(nine):
        at = i * halo
        halo_out[0, at : at + halo] = ref[i, TOP : TOP + halo]
        halo_out[1, at : at + halo] = ref[i, TOP + rows - halo : TOP + rows]

    inside = jnp.logical_and(has_low, has_high)

    @pl.when(inside)
    def _():
        pl.semaphore_wait(barrier, tms + 1)

    @pl.when(jnp.logical_not(inside))
    def _():
        pl.semaphore_wait(barrier, tms)

    to_below = pltpu.make_async_remote_copy(
        halo_out.at[0], halo_in.at[1], halo_send.at[0], halo_recv.at[1],
        device_id=(tm, strip - 1), device_id_type=MESH,
    )
    to_above = pltpu.make_async_remote_copy(
        halo_out.at[1], halo_in.at[0], halo_send.at[1], halo_recv.at[0],
        device_id=(tm, strip + 1), device_id_type=MESH,
    )

    across_above = lax.rem(strip, 2) == 0

    @pl.when(jnp.logical_and(has_low, across_above))
    def _():
        to_below.start()

    @pl.when(has_high)
    def _():
        to_above.start()

    @pl.when(jnp.logical_and(has_low, jnp.logical_not(across_above)))
    def _():
        to_below.start()

    def wait_for(slabs, sem):
        pltpu.make_async_copy(slabs, slabs, sem).wait()

    def spread_out(out, into, send, recv):
        copies = []
        for to in others_by(ORDER):
            copies.append(pltpu.make_async_remote_copy(
                out.at[to], into.at[tm], send, recv,
                device_id=(to, strip), device_id_type=MESH,
            ))
        for copy in copies:
            copy.start()
        into[tm] = out[tm]

    loads[0].wait()
    for p in range(3):
        regroup(0, p, fa, TOP, HALF if p == 0 else None)
    for n, buf in ((2, spread), (3, decay)):
        loads[n + 1].wait()
        for p in range(3):
            regroup(n, p, buf, 0, None)
    for i in range(nine):
        for j in range(tms):
            here = slice(per * j, per * (j + 1))
            inc_out[j, per * i : per * (i + 1)] = fa[i, TOP + per * j : TOP + per * (j + 1)]
            pre_out[j, per * i : per * (i + 1)] = spread[i, here]
            pre_out[j, flat + per * i : flat + per * (i + 1)] = decay[i, here]
    to_mate = pltpu.make_async_remote_copy(
        inc_out, mate, mate_send, mate_recv, device_id=(jnp.maximum(tm - 1, 0), strip), device_id_type=MESH
    )

    @pl.when(odd)
    def _():
        to_mate.start()
        mate[...] = jnp.zeros_like(mate)

    @pl.when(even)
    def _():
        spread_out(inc_out, inc_in, inc_send, inc_recv)

    spread_out(pre_out, pre_in, pre_send, pre_recv)

    @pl.when(has_low)
    def _():
        to_above.wait_recv()
        for i in range(nine):
            ref[i, TOP - halo : TOP] = halo_in[0, i * halo : (i + 1) * halo]

    @pl.when(has_high)
    def _():
        to_below.wait_recv()
        for i in range(nine):
            ref[i, TOP + rows : TOP + rows + halo] = halo_in[1, i * halo : (i + 1) * halo]

    run_steps(tangent_tile, tangent_products, bufs, ref, fc, rows, has_low, has_high, True)
    for i in range(nine):
        for q in range(edge):
            at = slice(per * i, per * (i + 1))
            beside_out[tms - edge + q, at] = fa[i, TOP - halo + per * q : TOP - halo + per * (q + 1)]
            beside_out[q, at] = fa[i, TOP + rows + per * q : TOP + rows + per * (q + 1)]

    def to_beside(to, beside):
        return pltpu.make_async_remote_copy(
            beside_out.at[to], beside_in.at[tm], beside_send, beside_recv,
            device_id=(to, beside), device_id_type=MESH,
        )

    @pl.when(has_low)
    def _():
        for n in range(edge):
            to_beside(tms - edge + lax.rem(tm + n, edge), strip - 1).start()

    @pl.when(has_high)
    def _():
        for n in range(edge):
            to_beside(lax.rem(tm + n, edge), strip + 1).start()

    @pl.when(even)
    def _():
        to_mate.wait_recv()

    for i in range(nine):
        for j in range(tms):
            at = slice(per * i, per * (i + 1))
            tan_out[j, at] = mate[j, at] - fa[i, TOP + per * j : TOP + per * (j + 1)]

    spread_out(tan_out, tan_in, tan_send, tan_recv)

    others = pl.ds(0, tms - 1)
    wait_for(pre_in.at[others], pre_recv)

    @pl.when(even)
    def _():
        wait_for(inc_in.at[pl.ds(0, tms // 2 - 1)], inc_recv)

    @pl.when(odd)
    def _():
        wait_for(inc_in.at[pl.ds(0, tms // 2)], inc_recv)

    wait_for(tan_in.at[others], tan_recv)
    @pl.when(jnp.logical_or(to_low, to_high))
    def _():
        wait_for(beside_in, beside_recv)

    built = None
    for k in range(tms):
        if k == 0:
            residual = inc_in[k]
        else:
            residual = tan_in[k - 1] - beside_in[k - 1]
            if k % 2 == 0:
                residual = inc_in[k] + residual
        scaled = pre_in[k, 0:flat] * residual
        built = scaled if k == 0 else pre_in[k, flat:] * built + scaled
        scan_b[k] = built
    w_own[tms] = jnp.zeros((flat, LANES), jnp.float32)
    smoothed = None
    for k in reversed(range(tms)):
        smoothed = scan_b[k] if smoothed is None else scan_b[k] + pre_in[k + 1, flat:] * smoothed
        w_own[k] = pre_in[k, 0:flat] * smoothed

    def to_low_halo(to):
        return pltpu.make_async_remote_copy(
            w_own.at[to + 1], wh_in.at[lax.rem(tm, edge)], wh_send, wh_recv,
            device_id=(to, strip - 1), device_id_type=MESH,
        )

    def to_high_halo(to):
        at = lax.rem(tm + edge - (tms - edge) % edge, edge)
        return pltpu.make_async_remote_copy(
            w_own.at[to + 1], wl_in.at[at], wh_send, wl_recv,
            device_id=(to, strip + 1), device_id_type=MESH,
        )

    def to_same(to, shift, into, send, recv):
        return pltpu.make_async_remote_copy(
            w_own.at[to + shift], into.at[tm], send, recv, device_id=(to, strip), device_id_type=MESH
        )

    for ways, halo_ways in RETURN:
        @pl.when(to_low)
        def _():
            for way in halo_ways:
                to_low_halo(partner(*way)).start()

        @pl.when(to_high)
        def _():
            for way in halo_ways:
                to_high_halo(partner(*way)).start()

        for to in others_by(ways):
            to_same(to, 1, w_in, w_send, w_recv).start()
    for to in others_by(ORDER):
        to_same(to, 0, wk_in, wk_send, wk_recv).start()
    w_in[tm] = w_own[tm + 1]
    wk_in[tm] = w_own[tm]

    @pl.when(jnp.logical_not(has_low))
    def _():
        fa[:, TOP - 16 : TOP] = jnp.zeros((nine, 16, LANES), jnp.float32)

    @pl.when(jnp.logical_not(has_high))
    def _():
        fa[:, TOP + rows : TOP + rows + 16] = jnp.zeros((nine, 16, LANES), jnp.float32)

    def unpack(slab, at):
        for i in range(nine):
            part = slab[per * i : per * (i + 1)]
            fa[i, at : at + per] = part * (1.0 / HALF**2) if i < cols else part

    wait_for(w_in.at[others], w_recv)
    for j in range(tms):
        unpack(w_in.at[j], TOP + per * j)

    @pl.when(has_low)
    def _():
        wait_for(wl_in, wl_recv)
        for q in range(edge):
            unpack(wl_in.at[q], TOP - halo + per * q)

    @pl.when(has_high)
    def _():
        wait_for(wh_in, wh_recv)
        for q in range(edge):
            unpack(wh_in.at[q], TOP + rows + per * q)

    run_steps(adjoint_tile, adjoint_products, bufs, ref, fc, rows, has_low, has_high, False)
    wait_for(wk_in.at[others], wk_recv)
    for j in range(tms):
        for i in range(nine):
            wk[i, per * j : per * (j + 1)] = wk_in[j, per * i : per * (i + 1)]
    for p in range(3):
        for t in range(rows // 8):
            at = pl.ds(8 * t, 8)
            parts = []
            for j in range(cols):
                weighted, adjoint = wk[p * cols + j, at], fa[p * cols + j, pl.ds(TOP + 8 * t, 8)]
                if p == 0:
                    weighted, adjoint = weighted * (1.0 / HALF), adjoint * HALF
                parts.append(take_lanes(weighted - adjoint, back[j]))
            for c in range(cols):
                out_ref[0, p, at, c * LANES : (c + 1) * LANES] = choose(marks, parts, c)

    @pl.when(has_low)
    def _():
        wait_for(beside_out.at[pl.ds(0, edge)], beside_send)

    @pl.when(has_high)
    def _():
        wait_for(beside_out.at[pl.ds(0, edge)], beside_send)

    @pl.when(has_low)
    def _():
        to_below.wait_send()

    @pl.when(has_high)
    def _():
        to_above.wait_send()

    @pl.when(jnp.logical_or(to_low, to_high))
    def _():
        wait_for(w_own.at[pl.ds(0, tms)], wh_send)

    @pl.when(even)
    def _():
        wait_for(inc_out.at[others], inc_send)

    @pl.when(odd)
    def _():
        to_mate.wait_send()

    for slabs, sem in ((pre_out, pre_send), (tan_out, tan_send), (w_own, w_send), (w_own, wk_send)):
        wait_for(slabs.at[others], sem)


def body(tms, strips, increment, ref_depth, ref_wind, spread, decay):
    _, planes, rows, width = increment.shape
    cols = width // LANES
    nine = planes * cols
    per = rows // tms
    flat = per * nine
    edge = STEPS // per
    height = rows + 2 * TOP
    edge_rows = -(-nine * STEPS // 8) * 8
    dma = pltpu.SemaphoreType.DMA
    f32 = jnp.float32
    vmem = lambda *shape: pltpu.VMEM(shape, f32)
    hbm = pl.BlockSpec(memory_space=pl.ANY)
    return pl.pallas_call(
        functools.partial(kernel, tms, strips, strips * rows),
        out_shape=jax.ShapeDtypeStruct(increment.shape, f32),
        in_specs=[hbm] * 5,
        out_specs=pl.BlockSpec(memory_space=pltpu.VMEM),
        scratch_shapes=[
            vmem(4, planes, rows, width),
            vmem(nine, height, LANES), vmem(nine, height, LANES), vmem(nine, height, LANES),
            vmem(2 * cols, height, LANES), vmem(2 * cols, height, LANES), vmem(height, LANES),
            vmem(nine, rows, LANES), vmem(nine, rows, LANES),
            vmem(2, edge_rows, LANES), vmem(2, edge_rows, LANES),
            vmem(tms, 2 * flat, LANES), vmem(tms, 2 * flat, LANES),
            vmem(tms, flat, LANES), vmem(tms, flat, LANES), vmem(tms, flat, LANES),
            vmem(tms, flat, LANES), vmem(tms, flat, LANES), vmem(tms, flat, LANES), vmem(tms, flat, LANES),
            vmem(tms, flat, LANES), vmem(tms + 1, flat, LANES), vmem(tms, flat, LANES),
            vmem(edge, flat, LANES), vmem(edge, flat, LANES), vmem(tms, flat, LANES),
            vmem(nine, rows, LANES),
            dma((5,)), dma((2,)), dma((2,)), *[dma] * 17,
        ],
        compiler_params=pltpu.CompilerParams(
            collective_id=0, has_side_effects=True, vmem_limit_bytes=24 * 2**20
        ),
    )(*(pltpu.with_memory_space_constraint(x, pltpu.HBM) for x in (increment, ref_depth, ref_wind, spread, decay)))


def solution(mesh):
    spec = P("tm", None, "strip", None)
    return jax.shard_map(
        functools.partial(body, mesh.shape["tm"], mesh.shape["strip"]),
        mesh=mesh,
        in_specs=(spec,) * 5,
        out_specs=spec,
        check_vma=False,
    )
```

```python
import functools

import jax
import jax.numpy as jnp
from jax import lax
from jax.experimental import pallas as pl
from jax.experimental.pallas import tpu as pltpu
from jax.sharding import PartitionSpec as P

STEPS = 12
DT = 0.4
HALF = 0.5 * DT
LANES = 128
TOP = 24
MESH = pl.DeviceIdType.MESH
ORDER = [(dy, dx, dc) for dx in (0, 1) for dy in (2, 1, 3, 0) for dc in (0, 1)]
NEAR, FAR = ORDER[:8], ORDER[8:]
RETURN = ((FAR, NEAR), (NEAR, FAR))


def diff_x(f):
    after = pltpu.roll(f[:1], LANES - 1, 2)
    before = pltpu.roll(f[-1:], 1, 2)
    return jnp.concatenate([f[1:], after], axis=0) - jnp.concatenate([before, f[:-1]], axis=0)


def third(x):
    return (x * 21846) >> 16


def column_maps(cols):
    lane = lax.broadcasted_iota(jnp.int32, (8, LANES), 1)
    rest = lane - cols * third(lane)
    into, back = [], []
    for j in range(cols):
        x = cols * lane + j
        into.append(x & (LANES - 1))
        block = rest + 2 * j
        block = block - cols * third(block)
        back.append(third(LANES * block + lane - j))
    return (rest == 0, rest == 1), into, back


def choose(marks, parts, j):
    pick = [parts[(2 * j + r) % len(parts)] for r in range(3)]
    return jnp.where(marks[0], pick[0], jnp.where(marks[1], pick[1], pick[2]))


def take_lanes(x, index):
    return jnp.take_along_axis(x, index, axis=1, mode="promise_in_bounds")


def tangent_products(new, ref, rows, tmp):
    cols = tmp.shape[0] // 2
    tmp[:cols, rows] = ref[0:cols, rows] * new[2] + ref[2 * cols :, rows] * new[0]


def tangent_tile(src, ref, tmp, fc, at):
    cols = src.shape[0] // 3
    rows, below, above = (pl.ds(at + d, 8) for d in (0, -1, 1))

    def diff_y(buf, i):
        return buf[i * cols : (i + 1) * cols, above] - buf[i * cols : (i + 1) * cols, below]

    h, u, v = (src[i * cols : (i + 1) * cols, rows] for i in range(3))
    depth, east, north = (ref[i * cols : (i + 1) * cols, rows] for i in range(3))
    turn = fc[rows][None]
    flux = depth * u + east * h
    new_h = h - (diff_x(flux) + diff_y(tmp, 0))
    new_u = u - ((east * diff_x(u) + north * diff_y(src, 1)) + (diff_x(h) - turn * v))
    new_v = v - ((east * diff_x(v) + north * diff_y(src, 2)) + (diff_y(src, 0) + turn * u))
    return new_h, new_u, new_v


def adjoint_products(new, ref, rows, tmp):
    cols = tmp.shape[0] // 2
    north = ref[2 * cols :, rows]
    tmp[:cols, rows] = north * new[1]
    tmp[cols:, rows] = north * new[2]


def adjoint_tile(src, ref, tmp, fc, at):
    cols = src.shape[0] // 3
    rows, below, above = (pl.ds(at + d, 8) for d in (0, -1, 1))

    def diff_y(buf, i):
        return buf[i * cols : (i + 1) * cols, above] - buf[i * cols : (i + 1) * cols, below]

    p, q, s = (src[i * cols : (i + 1) * cols, rows] for i in range(3))
    depth, east, north = (ref[i * cols : (i + 1) * cols, rows] for i in range(3))
    turn = fc[rows][None]
    px, py = diff_x(p), diff_y(src, 0)
    new_p = p + ((east * px + north * py) + (diff_x(q) + diff_y(src, 2)))
    new_q = q + ((depth * px - turn * s) + (diff_x(east * q) + diff_y(tmp, 0)))
    new_s = s + ((depth * py + turn * q) + (diff_x(east * s) + diff_y(tmp, 1)))
    return new_p, new_q, new_s


def run_steps(tile, products, bufs, ref, fc, rows, has_low, has_high, spreads):
    lo, hi = TOP // 8, (TOP + rows) // 8
    cols = ref.shape[0] // 3

    reach = 1 if spreads else 2
    for t in range(lo - reach, hi + reach):
        at = pl.ds(8 * t, 8)
        products([bufs[0][0][i * cols : (i + 1) * cols, at] for i in range(3)], ref, at, bufs[0][1])

    def step(j, more, last=False):
        (src, tmp), (dst, new_tmp) = bufs if j % 2 else bufs[::-1]
        for t in range(lo - more, hi + more):
            new = tile(src, ref, tmp, fc, 8 * t)
            if t == lo - 1:
                new = [jnp.where(has_low, x, 0.0) for x in new]
            if t == hi:
                new = [jnp.where(has_high, x, 0.0) for x in new]
            at = pl.ds(8 * t, 8)
            for i, x in enumerate(new):
                dst[i * cols : (i + 1) * cols, at] = x
            if not last:
                products(new, ref, at, new_tmp)

    def four(first):
        def turn(_, carry):
            for j in range(first, first + 4):
                step(j, 1)
            return carry

        lax.fori_loop(0, 2, turn, 0)

    if spreads:
        four(1)
        for j in range(9, STEPS + 1):
            step(j, 2, last=j == STEPS)
    else:
        for j in (1, 2, 3):
            step(j, 2)
        four(4)
        step(STEPS, 0, last=True)


def kernel(
    tms, strips, total_rows,
    inc_hbm, depth_hbm, wind_hbm, spread_hbm, decay_hbm, out_ref,
    raw, fa, fb, ref, tmp_a, tmp_b, fc, spread, decay,
    halo_out, halo_in, pre_out, pre_in, inc_out, inc_in, mate, tan_out, tan_in, beside_out, beside_in, scan_b, w_own, w_in, wl_in, wh_in, wk_in, wk,
    load_sem, halo_send, halo_recv, pre_send, pre_recv, inc_send, inc_recv, mate_send, mate_recv, tan_send, tan_recv, beside_send, beside_recv,
    w_send, w_recv, wh_send, wl_recv, wh_recv, wk_send, wk_recv,
):
    nine = fa.shape[0]
    cols = nine // 3
    rows = spread.shape[1]
    per = rows // tms
    flat = per * nine
    bufs = ((fa, tmp_a), (fb, tmp_b))
    halo = STEPS
    edge = halo // per
    tm = lax.axis_index("tm")
    strip = lax.axis_index("strip")
    has_low, has_high = strip > 0, strip < strips - 1
    even, odd = lax.rem(tm, 2) == 0, lax.rem(tm, 2) == 1
    to_low, to_high = jnp.logical_and(has_low, tm < edge), jnp.logical_and(has_high, tm >= tms - edge)

    def partner(dy, dx, dc):
        y, x, c = lax.div(tm, 4), lax.rem(lax.div(tm, 2), 2), lax.rem(tm, 2)
        return 4 * lax.rem(y + dy, tms // 4) + 2 * (1 - x if dx else x) + (1 - c if dc else c)

    def others_by(order):
        return [partner(*way) for way in order if way != (0, 0, 0)]

    barrier = pltpu.get_barrier_semaphore()

    @pl.when(has_low)
    def _():
        pl.semaphore_signal(barrier, inc=1, device_id=(tm, strip - 1), device_id_type=MESH)

    @pl.when(has_high)
    def _():
        pl.semaphore_signal(barrier, inc=1, device_id=(tm, strip + 1), device_id_type=MESH)

    for d in range(1, tms):
        pl.semaphore_signal(barrier, inc=1, device_id=(lax.rem(tm + d, tms), strip), device_id_type=MESH)

    loads = [
        pltpu.make_async_copy(hbm.at[0], buf, load_sem.at[n])
        for n, (hbm, buf) in enumerate((
            (inc_hbm, raw.at[0]), (depth_hbm, raw.at[1, 0:1]), (wind_hbm, raw.at[1, 1:3]),
            (spread_hbm, raw.at[2]), (decay_hbm, raw.at[3]),
        ))
    ]
    for copy in loads:
        copy.start()

    marks, into, back = column_maps(cols)
    own = pl.ds(TOP, rows)

    def regroup(n, p, buf, offset, scale):
        for t in range(rows // 8):
            at = pl.ds(8 * t, 8)
            parts = [raw[n, p, at, c * LANES : (c + 1) * LANES] for c in range(cols)]
            for j in range(cols):
                new = take_lanes(choose(marks, parts, j), into[j])
                buf[p * cols + j, pl.ds(offset + 8 * t, 8)] = new * scale if scale else new

    for buf in (fa, fb, ref, tmp_a, tmp_b):
        nothing = jnp.zeros((buf.shape[0], 16, LANES), jnp.float32)
        buf[:, TOP - 16 : TOP] = nothing
        buf[:, TOP + rows : TOP + rows + 16] = nothing

    @pl.when(jnp.logical_not(jnp.logical_or(to_low, to_high)))
    def _():
        beside_in[...] = jnp.zeros_like(beside_in)

    row = lax.broadcasted_iota(jnp.int32, fc.shape, 0) + (strip * rows - TOP)
    fc[...] = DT * (0.2 + 0.4 * row.astype(jnp.float32) / total_rows)

    loads[1].wait()
    loads[2].wait()
    for p in range(3):
        regroup(1, p, ref, TOP, HALF * HALF if p == 0 else HALF)
    rest = halo_out.shape[1] - nine * halo
    halo_out[:, nine * halo :] = jnp.zeros((2, rest, LANES), jnp.float32)
    for i in range(nine):
        at = i * halo
        halo_out[0, at : at + halo] = ref[i, TOP : TOP + halo]
        halo_out[1, at : at + halo] = ref[i, TOP + rows - halo : TOP + rows]

    inside = jnp.logical_and(has_low, has_high)

    @pl.when(inside)
    def _():
        pl.semaphore_wait(barrier, tms + 1)

    @pl.when(jnp.logical_not(inside))
    def _():
        pl.semaphore_wait(barrier, tms)

    to_below = pltpu.make_async_remote_copy(
        halo_out.at[0], halo_in.at[1], halo_send.at[0], halo_recv.at[1],
        device_id=(tm, strip - 1), device_id_type=MESH,
    )
    to_above = pltpu.make_async_remote_copy(
        halo_out.at[1], halo_in.at[0], halo_send.at[1], halo_recv.at[0],
        device_id=(tm, strip + 1), device_id_type=MESH,
    )

    across_above = lax.rem(strip, 2) == 0

    @pl.when(jnp.logical_and(has_low, across_above))
    def _():
        to_below.start()

    @pl.when(has_high)
    def _():
        to_above.start()

    @pl.when(jnp.logical_and(has_low, jnp.logical_not(across_above)))
    def _():
        to_below.start()

    def wait_for(slabs, sem):
        pltpu.make_async_copy(slabs, slabs, sem).wait()

    def spread_out(out, into, send, recv):
        copies = []
        for to in others_by(ORDER):
            copies.append(pltpu.make_async_remote_copy(
                out.at[to], into.at[tm], send, recv,
                device_id=(to, strip), device_id_type=MESH,
            ))
        for copy in copies:
            copy.start()
        into[tm] = out[tm]

    loads[0].wait()
    for p in range(3):
        regroup(0, p, fa, TOP, HALF if p == 0 else None)
    for n, buf in ((2, spread), (3, decay)):
        loads[n + 1].wait()
        for p in range(3):
            regroup(n, p, buf, 0, None)
    for i in range(nine):
        for j in range(tms):
            here = slice(per * j, per * (j + 1))
            inc_out[j, per * i : per * (i + 1)] = fa[i, TOP + per * j : TOP + per * (j + 1)]
            pre_out[j, per * i : per * (i + 1)] = spread[i, here]
            pre_out[j, flat + per * i : flat + per * (i + 1)] = decay[i, here]
    to_mate = pltpu.make_async_remote_copy(
        inc_out, mate, mate_send, mate_recv, device_id=(jnp.maximum(tm - 1, 0), strip), device_id_type=MESH
    )

    @pl.when(odd)
    def _():
        to_mate.start()
        mate[...] = jnp.zeros_like(mate)

    @pl.when(even)
    def _():
        spread_out(inc_out, inc_in, inc_send, inc_recv)

    spread_out(pre_out, pre_in, pre_send, pre_recv)

    @pl.when(has_low)
    def _():
        to_above.wait_recv()
        for i in range(nine):
            ref[i, TOP - halo : TOP] = halo_in[0, i * halo : (i + 1) * halo]

    @pl.when(has_high)
    def _():
        to_below.wait_recv()
        for i in range(nine):
            ref[i, TOP + rows : TOP + rows + halo] = halo_in[1, i * halo : (i + 1) * halo]

    run_steps(tangent_tile, tangent_products, bufs, ref, fc, rows, has_low, has_high, True)
    for i in range(nine):
        for q in range(edge):
            at = slice(per * i, per * (i + 1))
            beside_out[tms - edge + q, at] = fa[i, TOP - halo + per * q : TOP - halo + per * (q + 1)]
            beside_out[q, at] = fa[i, TOP + rows + per * q : TOP + rows + per * (q + 1)]

    def to_beside(to, beside):
        return pltpu.make_async_remote_copy(
            beside_out.at[to], beside_in.at[tm], beside_send, beside_recv,
            device_id=(to, beside), device_id_type=MESH,
        )

    @pl.when(has_low)
    def _():
        @pl.loop(tms - edge, tms)
        def _(to):
            to_beside(to, strip - 1).start()

    @pl.when(has_high)
    def _():
        @pl.loop(0, edge)
        def _(to):
            to_beside(to, strip + 1).start()

    @pl.when(even)
    def _():
        to_mate.wait_recv()

    for i in range(nine):
        for j in range(tms):
            at = slice(per * i, per * (i + 1))
            tan_out[j, at] = mate[j, at] - fa[i, TOP + per * j : TOP + per * (j + 1)]

    spread_out(tan_out, tan_in, tan_send, tan_recv)

    others = pl.ds(0, tms - 1)
    wait_for(pre_in.at[others], pre_recv)

    @pl.when(even)
    def _():
        wait_for(inc_in.at[pl.ds(0, tms // 2 - 1)], inc_recv)

    @pl.when(odd)
    def _():
        wait_for(inc_in.at[pl.ds(0, tms // 2)], inc_recv)

    wait_for(tan_in.at[others], tan_recv)
    @pl.when(jnp.logical_or(to_low, to_high))
    def _():
        wait_for(beside_in, beside_recv)

    built = None
    for k in range(tms):
        if k == 0:
            residual = inc_in[k]
        else:
            residual = tan_in[k - 1] - beside_in[k - 1]
            if k % 2 == 0:
                residual = inc_in[k] + residual
        scaled = pre_in[k, 0:flat] * residual
        built = scaled if k == 0 else pre_in[k, flat:] * built + scaled
        scan_b[k] = built
    w_own[tms] = jnp.zeros((flat, LANES), jnp.float32)
    smoothed = None
    for k in reversed(range(tms)):
        smoothed = scan_b[k] if smoothed is None else scan_b[k] + pre_in[k + 1, flat:] * smoothed
        w_own[k] = pre_in[k, 0:flat] * smoothed

    def to_low_halo(to):
        return pltpu.make_async_remote_copy(
            w_own.at[to + 1], wh_in.at[lax.rem(tm, edge)], wh_send, wh_recv,
            device_id=(to, strip - 1), device_id_type=MESH,
        )

    def to_high_halo(to):
        at = lax.rem(tm + edge - (tms - edge) % edge, edge)
        return pltpu.make_async_remote_copy(
            w_own.at[to + 1], wl_in.at[at], wh_send, wl_recv,
            device_id=(to, strip + 1), device_id_type=MESH,
        )

    def to_same(to, shift, into, send, recv):
        return pltpu.make_async_remote_copy(
            w_own.at[to + shift], into.at[tm], send, recv, device_id=(to, strip), device_id_type=MESH
        )

    for ways, halo_ways in RETURN:
        @pl.when(to_low)
        def _():
            for way in halo_ways:
                to_low_halo(partner(*way)).start()

        @pl.when(to_high)
        def _():
            for way in halo_ways:
                to_high_halo(partner(*way)).start()

        for to in others_by(ways):
            to_same(to, 1, w_in, w_send, w_recv).start()
    for to in others_by(ORDER):
        to_same(to, 0, wk_in, wk_send, wk_recv).start()
    w_in[tm] = w_own[tm + 1]
    wk_in[tm] = w_own[tm]

    @pl.when(jnp.logical_not(has_low))
    def _():
        fa[:, TOP - 16 : TOP] = jnp.zeros((nine, 16, LANES), jnp.float32)

    @pl.when(jnp.logical_not(has_high))
    def _():
        fa[:, TOP + rows : TOP + rows + 16] = jnp.zeros((nine, 16, LANES), jnp.float32)

    def unpack(slab, at):
        for i in range(nine):
            part = slab[per * i : per * (i + 1)]
            fa[i, at : at + per] = part * (1.0 / HALF**2) if i < cols else part

    wait_for(w_in.at[others], w_recv)
    for j in range(tms):
        unpack(w_in.at[j], TOP + per * j)

    @pl.when(has_low)
    def _():
        wait_for(wl_in, wl_recv)
        for q in range(edge):
            unpack(wl_in.at[q], TOP - halo + per * q)

    @pl.when(has_high)
    def _():
        wait_for(wh_in, wh_recv)
        for q in range(edge):
            unpack(wh_in.at[q], TOP + rows + per * q)

    run_steps(adjoint_tile, adjoint_products, bufs, ref, fc, rows, has_low, has_high, False)
    wait_for(wk_in.at[others], wk_recv)
    for j in range(tms):
        for i in range(nine):
            wk[i, per * j : per * (j + 1)] = wk_in[j, per * i : per * (i + 1)]
    for p in range(3):
        for t in range(rows // 8):
            at = pl.ds(8 * t, 8)
            parts = []
            for j in range(cols):
                weighted, adjoint = wk[p * cols + j, at], fa[p * cols + j, pl.ds(TOP + 8 * t, 8)]
                if p == 0:
                    weighted, adjoint = weighted * (1.0 / HALF), adjoint * HALF
                parts.append(take_lanes(weighted - adjoint, back[j]))
            for c in range(cols):
                out_ref[0, p, at, c * LANES : (c + 1) * LANES] = choose(marks, parts, c)

    @pl.when(has_low)
    def _():
        wait_for(beside_out.at[pl.ds(0, edge)], beside_send)

    @pl.when(has_high)
    def _():
        wait_for(beside_out.at[pl.ds(0, edge)], beside_send)

    @pl.when(has_low)
    def _():
        to_below.wait_send()

    @pl.when(has_high)
    def _():
        to_above.wait_send()

    @pl.when(jnp.logical_or(to_low, to_high))
    def _():
        wait_for(w_own.at[pl.ds(0, tms)], wh_send)

    @pl.when(even)
    def _():
        wait_for(inc_out.at[others], inc_send)

    @pl.when(odd)
    def _():
        to_mate.wait_send()

    for slabs, sem in ((pre_out, pre_send), (tan_out, tan_send), (w_own, w_send), (w_own, wk_send)):
        wait_for(slabs.at[others], sem)


def body(tms, strips, increment, ref_depth, ref_wind, spread, decay):
    _, planes, rows, width = increment.shape
    cols = width // LANES
    nine = planes * cols
    per = rows // tms
    flat = per * nine
    edge = STEPS // per
    height = rows + 2 * TOP
    edge_rows = -(-nine * STEPS // 8) * 8
    dma = pltpu.SemaphoreType.DMA
    f32 = jnp.float32
    vmem = lambda *shape: pltpu.VMEM(shape, f32)
    hbm = pl.BlockSpec(memory_space=pl.ANY)
    return pl.pallas_call(
        functools.partial(kernel, tms, strips, strips * rows),
        out_shape=jax.ShapeDtypeStruct(increment.shape, f32),
        in_specs=[hbm] * 5,
        out_specs=pl.BlockSpec(memory_space=pltpu.VMEM),
        scratch_shapes=[
            vmem(4, planes, rows, width),
            vmem(nine, height, LANES), vmem(nine, height, LANES), vmem(nine, height, LANES),
            vmem(2 * cols, height, LANES), vmem(2 * cols, height, LANES), vmem(height, LANES),
            vmem(nine, rows, LANES), vmem(nine, rows, LANES),
            vmem(2, edge_rows, LANES), vmem(2, edge_rows, LANES),
            vmem(tms, 2 * flat, LANES), vmem(tms, 2 * flat, LANES),
            vmem(tms, flat, LANES), vmem(tms, flat, LANES), vmem(tms, flat, LANES),
            vmem(tms, flat, LANES), vmem(tms, flat, LANES), vmem(tms, flat, LANES), vmem(tms, flat, LANES),
            vmem(tms, flat, LANES), vmem(tms + 1, flat, LANES), vmem(tms, flat, LANES),
            vmem(edge, flat, LANES), vmem(edge, flat, LANES), vmem(tms, flat, LANES),
            vmem(nine, rows, LANES),
            dma((5,)), dma((2,)), dma((2,)), *[dma] * 17,
        ],
        compiler_params=pltpu.CompilerParams(
            collective_id=0, has_side_effects=True, vmem_limit_bytes=24 * 2**20
        ),
    )(*(pltpu.with_memory_space_constraint(x, pltpu.HBM) for x in (increment, ref_depth, ref_wind, spread, decay)))


def solution(mesh):
    spec = P("tm", None, "strip", None)
    return jax.shard_map(
        functools.partial(body, mesh.shape["tm"], mesh.shape["strip"]),
        mesh=mesh,
        in_specs=(spec,) * 5,
        out_specs=spec,
        check_vma=False,
    )
```
